32 devices in a mesh: dp: 8 (over z, x), seq: 4 (over y, core).
Axes of the slice: x: 2, y: 2, z: 4, core: 2. Of those that a mesh axis runs over, the one named last changes fastest.
Arguments:
- block_input: bfloat16 [8, 1024, 1472], P('dp', 'seq'), may hold values from -6 to 6
- segment_ids: int32 [8, 1024], P('dp'), may hold values from 0 to 7, never falling along the last dimension, each value on 1 to 768 neighbouring positions
- attention_gain: float32 [1472], replicated, may hold values from 0.5 to 1.5
- query_weight: bfloat16 [565248], P(('dp', 'seq')), may hold values from -0.0390625 to 0.0390625
- key_weight: bfloat16 [565248], P(('dp', 'seq')), may hold values from -0.15625 to 0.15625
- value_weight: bfloat16 [565248], P(('dp', 'seq')), may hold values from -0.15625 to 0.15625
- output_weight: bfloat16 [565248], P(('dp', 'seq')), may hold values from -1.75 to 1.75
- bias_table: float32 [32, 6], replicated, may hold values from -3 to 3
- feedforward_gain: float32 [1472], replicated, may hold values from 0.5 to 1.5
- gelu_weight: bfloat16 [5275648], P(('dp', 'seq')), may hold values from -0.15625 to 0.15625
- up_weight: bfloat16 [5275648], P(('dp', 'seq')), may hold values from -0.15625 to 0.15625
- down_weight: bfloat16 [5275648], P(('dp', 'seq')), may hold values from -0.125 to 0.125
- delete_gain: float32 [1472], replicated, may hold values from 0.5 to 1.5
- delete_weight: float32 [1472], replicated, may hold values from -0.15625 to 0.15625
- delete_bias: float32 [1], replicated, may hold values from -3 to 3
- output_cotangent: bfloat16 [8, 1024, 1472], P('dp', 'seq'), may hold values from -6 to 6
- gate_cotangent: float32 [8, 1024], P('dp', 'seq'), may hold values from -0.6 to 0.6
Outputs:
- block_output: bfloat16 [8, 1024, 1472], P('dp', 'seq')
- delete_gate: float32 [8, 1024], P('dp', 'seq')
- input_gradient: float32 [8, 1024, 1472], P('dp', 'seq')
- attention_gain_gradient: float32 [1472], replicated
- query_weight_gradient: float32 [565248], P(('dp', 'seq'))
- key_weight_gradient: float32 [565248], P(('dp', 'seq'))
- value_weight_gradient: float32 [565248], P(('dp', 'seq'))
- output_weight_gradient: float32 [565248], P(('dp', 'seq'))
- bias_table_gradient: float32 [32, 6], replicated
- feedforward_gain_gradient: float32 [1472], replicated
- gelu_weight_gradient: float32 [5275648], P(('dp', 'seq'))
- up_weight_gradient: float32 [5275648], P(('dp', 'seq'))
- down_weight_gradient: float32 [5275648], P(('dp', 'seq'))
- delete_gain_gradient: float32 [1472], replicated
- delete_weight_gradient: float32 [1472], replicated
- delete_bias_gradient: float32 [1], replicated
The draws below stay inside these ranges and needn't reach their ends.
Inputs may be any that keep to these rules, and one draw needn't show every extreme that they name: `segment_ids`: within each row the numbers never fall and every one of the 8 documents is a run of 1 to 768 positions, one of them exactly that long.
All inputs are finite; a program needn't handle non-finite values.
Results may differ from the reference program's by a relative error of at most 0.015.
The reference program's roundings to bfloat16 on the way count: a program that leaves them out, or rounds other values in their place, can miss the bound.
Values may be sent and summed in bfloat16 or wider, within the bound.
A program may use at most 384 MiB of HBM per device.

```python
import math
import jax
import jax.numpy as jnp
import numpy as np
from jax import lax

D = 1472
HEADS = 6
HEAD_DIM = 64
FF = 3584
BUCKETS = 32
MAX_DIST = 128
DOCS = 8
INNER = 384
LEN = 1024
ROWS = 8


def steps_of(key, dims, cuts, least, top_value):
    level = 1.0
    for axis_at, parts in cuts:
        heights = jax.random.uniform(jax.random.fold_in(jax.random.fold_in(key, 6), axis_at), (parts,), jnp.float32, least / len(cuts), top_value / len(cuts))
        level = level * jnp.repeat(jnp.exp(heights), dims[axis_at] // parts).reshape((-1,) + (1,) * (len(dims) - 1 - axis_at))
    return level


def profile(amount, total, most, lean):
    loads = [(1 << 20) // math.isqrt(standing ** lean) + 1 for standing in range(2, amount + 1)]
    spare, counts = total - most - (amount - 1), [1] * (amount - 1)
    while spare > 0:
        movable = [i for i in range(amount - 1) if counts[i] < most]
        mass, budget = sum([loads[i] for i in movable]), spare
        for i in movable:
            more = min(most - counts[i], max(1, budget * loads[i] // mass), spare)
            counts[i] = counts[i] + more
            spare = spare - more
    return np.array([most] + counts)


def ragged_sizes(own_key, number_of, total, bound, slope):
    if number_of == 2:
        one = jax.random.randint(own_key, (), max(1, total - bound), min(bound, total - 1) + 1)
        return jnp.stack([one, total - one])
    sizes = jnp.asarray(profile(number_of, total, bound, slope), jnp.int32)
    twos = (number_of - 1) // 2
    donor, taker = sizes[1:1 + 2 * twos:2], sizes[2:2 + 2 * twos:2]
    room = jnp.minimum(donor - 1, bound - taker)
    shifted = jax.random.randint(jax.random.fold_in(own_key, 1), (twos,), 0, 1 << 20) % (room + 1)
    sizes = sizes.at[1:1 + 2 * twos:2].set(donor - shifted).at[2:2 + 2 * twos:2].set(taker + shifted)
    return sizes[jax.random.permutation(jax.random.fold_in(own_key, 2), number_of)]


def normal_values(key, extent, scale, most, shards=(), kind=jnp.bfloat16):
    entries = scale * jax.random.normal(key, extent, jnp.float32)
    if shards:
        entries = entries * steps_of(key, extent, shards, -0.22, 0.18)
    return jnp.clip(entries, -most, most).astype(kind)


def setup_inputs(seed: int = 0) -> dict:
    arg_keys = jax.random.split(jax.random.key(seed), 18)
    return {
        "block_input": normal_values(arg_keys[0], (ROWS, LEN, D), 1.0, 6.0, ((0, 8), (1, 4))),
        "segment_ids": jax.vmap(lambda own: jnp.searchsorted(jnp.cumsum(ragged_sizes(own, DOCS, LEN, 3 * LEN // 4, 0)), jnp.arange(LEN), side="right"))(jax.random.split(arg_keys[1], ROWS)).reshape((ROWS, LEN)).astype(jnp.int32),
        "attention_gain": jnp.clip(1.0 + 0.1 * jax.random.normal(arg_keys[2], (D,), jnp.float32), 0.5, 1.5),
        "query_weight": normal_values(arg_keys[3], (D * INNER,), (16 * D) ** -0.5, 0.0390625, ((0, 32),)),
        "key_weight": normal_values(arg_keys[4], (D * INNER,), D ** -0.5, 0.15625, ((0, 32),)),
        "value_weight": normal_values(arg_keys[5], (D * INNER,), D ** -0.5, 0.15625, ((0, 32),)),
        "output_weight": normal_values(arg_keys[6], (INNER * D,), (INNER // 32) ** -0.5, 1.75, ((0, 32),)),
        "bias_table": normal_values(arg_keys[7], (BUCKETS, HEADS), 1.0, 3.0, (), jnp.float32),
        "feedforward_gain": jnp.clip(1.0 + 0.1 * jax.random.normal(arg_keys[8], (D,), jnp.float32), 0.5, 1.5),
        "gelu_weight": normal_values(arg_keys[9], (D * FF,), D ** -0.5, 0.15625, ((0, 32),)),
        "up_weight": normal_values(arg_keys[10], (D * FF,), D ** -0.5, 0.15625, ((0, 32),)),
        "down_weight": normal_values(arg_keys[11], (FF * D,), (FF // 2) ** -0.5, 0.125, ((0, 32),)),
        "delete_gain": jnp.clip(1.0 + 0.1 * jax.random.normal(arg_keys[12], (D,), jnp.float32), 0.5, 1.5),
        "delete_weight": normal_values(arg_keys[13], (D,), D ** -0.5, 0.15625, (), jnp.float32),
        "delete_bias": normal_values(arg_keys[14], (1,), 1.0, 3.0, (), jnp.float32),
        "output_cotangent": normal_values(arg_keys[15], (ROWS, LEN, D), 1.0, 6.0, ((0, 8), (1, 4))),
        "gate_cotangent": normal_values(arg_keys[16], (ROWS, LEN), 0.1, 0.6, ((0, 8), (1, 4)), jnp.float32),
    }


EPS = 1e-06
HIGH = lax.Precision.HIGHEST
SLOPE = 0.7978845608028654
CUBIC = 0.044715
DEPTH = -30.0

@jax.custom_vjp
def low(v):
    return lax.optimization_barrier(v.astype(jnp.bfloat16)).astype(jnp.float32)

@jax.custom_vjp
def low_back(v):
    return v

def low_keep(v):
    return (low(v), None)

def low_pass(kept, grad):
    return (grad,)

def back_keep(v):
    return (v, None)

def back_low(kept, grad):
    return (low(grad),)
low.defvjp(low_keep, low_pass)
low_back.defvjp(back_keep, back_low)

def relative_buckets(length, buckets, reach):
    half = buckets // 2
    exact = half // 2
    offsets = np.arange(-(length - 1), length)
    distance = np.abs(offsets)
    safe_far = np.maximum(distance, 1)
    spread = exact + np.floor(np.log(safe_far / exact) / math.log(reach / exact) * (half - exact)).astype(np.int32)
    spread = np.minimum(spread, half - 1)
    chosen = np.where(distance < exact, distance, spread) + np.where(offsets > 0, half, 0)
    return chosen.astype(np.int32)

def normalize(value, gain):
    return value * lax.rsqrt(lax.optimization_barrier(jnp.mean(value * value, axis=-1, keepdims=True)) + EPS) * gain

def matmul_high(left, right):
    return jnp.dot(left, right, precision=HIGH)

def gelu_tanh(value):
    return 0.5 * value * (1.0 + jnp.tanh(SLOPE * (value + CUBIC * value * value * value)))

def block_forward(params, row_block, doc_ids, bucket_ids, offset_ids):
    gain_one, w_query, w_key, w_value, w_out, table, gain_two, w_gelu, w_up, w_down, gain_three, w_delete, b_delete = params
    groups = row_block.shape[0]
    length = row_block.shape[1]
    normed_one = low(normalize(row_block, gain_one))
    query = low_back(low(matmul_high(normed_one, w_query))).reshape(groups, length, HEADS, HEAD_DIM)
    keys = low_back(low(matmul_high(normed_one, w_key))).reshape(groups, length, HEADS, HEAD_DIM)
    values = low_back(low(matmul_high(normed_one, w_value))).reshape(groups, length, HEADS, HEAD_DIM)
    per_offset = jnp.take(table, bucket_ids, axis=0)
    bias_full = jnp.transpose(jnp.take(per_offset, offset_ids, axis=0), (2, 0, 1))
    scores = low_back(jnp.einsum('gqhd,gkhd->ghqk', query, keys, precision=HIGH)) + bias_full[None]
    allowed = (doc_ids[:, :, None] == doc_ids[:, None, :])[:, None]
    scores = jnp.where(allowed, scores, -1e+30)
    peak = lax.optimization_barrier(jnp.max(scores, axis=-1, keepdims=True))
    expo = jnp.exp(scores - peak)
    probs = expo / lax.optimization_barrier(jnp.sum(expo, axis=-1, keepdims=True))
    mixed = jnp.einsum('ghqk,gkhd->gqhd', low(probs), values, precision=HIGH)
    mixed = low_back(low(mixed.reshape(groups, length, INNER)))
    after_attn = row_block + low_back(matmul_high(mixed, w_out))
    normed_two = low(normalize(after_attn, gain_two))
    gate_pre = low_back(matmul_high(normed_two, w_gelu))
    up_pre = low_back(matmul_high(normed_two, w_up))
    hidden = low(gelu_tanh(gate_pre) * up_pre)
    after_ffn = after_attn + low_back(matmul_high(hidden, w_down))
    normed_three = normalize(after_ffn, gain_three)
    logits = matmul_high(normed_three, w_delete) + b_delete[0]
    return (after_ffn, DEPTH * jax.nn.sigmoid(logits))

def reference(block_input, segment_ids, attention_gain, query_weight, key_weight, value_weight, output_weight, bias_table, feedforward_gain, gelu_weight, up_weight, down_weight, delete_gain, delete_weight, delete_bias, output_cotangent, gate_cotangent):
    params = (attention_gain, query_weight.astype(jnp.float32).reshape(D, INNER), key_weight.astype(jnp.float32).reshape(D, INNER), value_weight.astype(jnp.float32).reshape(D, INNER), output_weight.astype(jnp.float32).reshape(INNER, D), bias_table, feedforward_gain, gelu_weight.astype(jnp.float32).reshape(D, FF), up_weight.astype(jnp.float32).reshape(D, FF), down_weight.astype(jnp.float32).reshape(FF, D), delete_gain, delete_weight, delete_bias)
    bucket_ids = jnp.asarray(relative_buckets(LEN, BUCKETS, MAX_DIST))
    positions = np.arange(LEN)
    offset_ids = jnp.asarray((positions[None, :] - positions[:, None] + LEN - 1).astype(np.int32))
    group_size = math.gcd(ROWS, max(1, 4096 // LEN))
    steps_count = ROWS // group_size
    inputs = block_input.astype(jnp.float32).reshape(steps_count, group_size, LEN, D)
    doc_blocks = segment_ids.reshape(steps_count, group_size, LEN)
    cot_blocks = output_cotangent.astype(jnp.float32).reshape(steps_count, group_size, LEN, D)
    gate_blocks = gate_cotangent.reshape(steps_count, group_size, LEN)

    def group_step(running, pieces):
        row_block, doc_ids, cot_out, cot_gate = pieces

        def forward_only(param_set, rows_in):
            return block_forward(param_set, rows_in, doc_ids, bucket_ids, offset_ids)
        outcome, pullback = jax.vjp(forward_only, params, row_block)
        param_grads, input_grads = pullback((cot_out, cot_gate))
        running = jax.tree.map(lambda before, addend: before + addend, running, param_grads)
        return (running, (outcome[0].astype(jnp.bfloat16), outcome[1], input_grads))
    zeros_start = jax.tree.map(jnp.zeros_like, params)
    totals, (outputs, gates, input_grads) = lax.scan(group_step, zeros_start, (inputs, doc_blocks, cot_blocks, gate_blocks))
    return (outputs.reshape(ROWS, LEN, D), gates.reshape(ROWS, LEN), input_grads.reshape(ROWS, LEN, D), totals[0], totals[1].reshape(-1), totals[2].reshape(-1), totals[3].reshape(-1), totals[4].reshape(-1), totals[5], totals[6], totals[7].reshape(-1), totals[8].reshape(-1), totals[9].reshape(-1), totals[10], totals[11], totals[12])
```

```python
import math

import jax
import jax.numpy as jnp
import numpy as np
from jax import lax
from jax.experimental import pallas as pl
from jax.experimental.pallas import tpu as pltpu
from jax.sharding import PartitionSpec as P

D = 1472
HEADS = 6
HEAD_DIM = 64
FF = 3584
BUCKETS = 32
MAX_DIST = 128
INNER = 384


EPS = 1e-06
HIGH = lax.Precision.HIGHEST
SLOPE = 0.7978845608028654
CUBIC = 0.044715
DEPTH = -30.0


def relative_buckets(length, buckets, reach):
    half = buckets // 2
    exact = half // 2
    offsets = np.arange(-(length - 1), length)
    distance = np.abs(offsets)
    safe_far = np.maximum(distance, 1)
    spread = exact + np.floor(
        np.log(safe_far / exact) / math.log(reach / exact) * (half - exact)
    ).astype(np.int32)
    spread = np.minimum(spread, half - 1)
    chosen = np.where(distance < exact, distance, spread) + np.where(offsets > 0, half, 0)
    return chosen.astype(np.int32)


def bucket_grid(length, buckets, reach):
    flat = relative_buckets(length, buckets, reach)
    places = np.arange(length)
    return flat[places[None, :] - places[:, None] + length - 1].astype(np.int32)


def gelu_tanh(value):
    return 0.5 * value * (1.0 + jnp.tanh(SLOPE * (value + CUBIC * value * value * value)))


def gelu_slope(value):
    tangent = jnp.tanh(SLOPE * (value + CUBIC * value * value * value))
    return 0.5 * (1.0 + tangent) + 0.5 * value * (1.0 - tangent * tangent) * SLOPE * (
        1.0 + 3.0 * CUBIC * value * value
    )


def norm_scale(value):
    return lax.rsqrt(jnp.mean(value * value, axis=-1, keepdims=True) + EPS)


def norm_back(value, scaling, gain, upstream):
    weighted = gain * upstream
    return scaling * weighted - value * (scaling * scaling * scaling) * jnp.mean(
        value * weighted, axis=-1, keepdims=True
    )


def project(inputs, gain, gathered):
    scale_one = norm_scale(inputs)
    normed_one = (inputs * scale_one * gain).astype(jnp.bfloat16)
    query = jnp.dot(
        normed_one, gathered[0].reshape(D, INNER), preferred_element_type=jnp.float32
    ).astype(jnp.bfloat16)
    keys = jnp.dot(
        normed_one, gathered[1].reshape(D, INNER), preferred_element_type=jnp.float32
    ).astype(jnp.bfloat16)
    values = jnp.dot(
        normed_one, gathered[2].reshape(D, INNER), preferred_element_type=jnp.float32
    ).astype(jnp.bfloat16)
    return (scale_one, normed_one, query, keys, values)


def forward_rest(
    inputs,
    projected,
    fetched,
    gathered,
    bias_full,
    allowed,
    feedforward_gain,
    delete_gain,
    delete_weight,
    delete_bias,
):
    query = projected[2]
    keys_all, values_all = fetched
    row_count = keys_all.shape[0]
    query_four = query.reshape(row_count, -1, HEADS, HEAD_DIM)
    keys_four = keys_all.reshape(row_count, -1, HEADS, HEAD_DIM)
    values_four = values_all.reshape(row_count, -1, HEADS, HEAD_DIM)
    scores = (
        jnp.einsum("rqhd,rkhd->rhqk", query_four, keys_four, preferred_element_type=jnp.float32)
        + bias_full[None]
    )
    scores = jnp.where(allowed, scores, -1e30)
    peak = jnp.max(scores, axis=-1, keepdims=True)
    expo = jnp.exp(scores - peak)
    probs = expo / jnp.sum(expo, axis=-1, keepdims=True)
    mixed = jnp.einsum(
        "rhqk,rkhd->rqhd",
        probs.astype(jnp.bfloat16),
        values_four,
        preferred_element_type=jnp.float32,
    )
    mixed = mixed.astype(jnp.bfloat16).reshape(-1, INNER)
    after_attn = inputs + jnp.dot(
        mixed, gathered[3].reshape(INNER, D), preferred_element_type=jnp.float32
    )
    scale_two = norm_scale(after_attn)
    normed_two = (after_attn * scale_two * feedforward_gain).astype(jnp.bfloat16)
    gate_pre = jnp.dot(normed_two, gathered[4].reshape(D, FF), preferred_element_type=jnp.float32)
    up_pre = jnp.dot(normed_two, gathered[5].reshape(D, FF), preferred_element_type=jnp.float32)
    hidden = (gelu_tanh(gate_pre) * up_pre).astype(jnp.bfloat16)
    after_ffn = after_attn + jnp.dot(
        hidden, gathered[6].reshape(FF, D), preferred_element_type=jnp.float32
    )
    scale_three = norm_scale(after_ffn)
    normed_three = after_ffn * scale_three * delete_gain
    logits = jnp.dot(normed_three, delete_weight, precision=HIGH) + delete_bias[0]
    return (
        probs,
        mixed,
        after_attn,
        scale_two,
        normed_two,
        gate_pre,
        up_pre,
        hidden,
        after_ffn,
        scale_three,
        normed_three,
        logits,
    )


def local(
    block_input,
    segment_ids,
    attention_gain,
    query_weight,
    key_weight,
    value_weight,
    output_weight,
    bias_table,
    feedforward_gain,
    gelu_weight,
    up_weight,
    down_weight,
    delete_gain,
    delete_weight,
    delete_bias,
    output_cotangent,
    gate_cotangent,
):
    row_count = block_input.shape[0]
    local_tokens = block_input.shape[1]
    seq_length = segment_ids.shape[1]
    offset = lax.axis_index("seq") * local_tokens
    inputs = block_input.astype(jnp.float32).reshape(-1, D)
    grid_all = jnp.asarray(bucket_grid(seq_length, BUCKETS, MAX_DIST))
    local_buckets = lax.dynamic_slice_in_dim(grid_all, offset, local_tokens, 0)
    one_hot = (local_buckets[:, :, None] == lax.iota(jnp.int32, BUCKETS)[None, None, :]).astype(
        jnp.float32
    )
    bias_full = jnp.einsum("qkb,bh->hqk", one_hot, bias_table, precision=HIGH)
    query_docs = lax.dynamic_slice_in_dim(segment_ids, offset, local_tokens, 1)
    allowed = (query_docs[:, :, None] == segment_ids[:, None, :])[:, None]
    shards = (
        query_weight,
        key_weight,
        value_weight,
        output_weight,
        gelu_weight,
        up_weight,
        down_weight,
    )
    gathered = (
        lax.all_gather(shards[0], ("dp", "seq"), axis=0, tiled=True),
        lax.all_gather(shards[1], ("dp", "seq"), axis=0, tiled=True),
        lax.all_gather(shards[2], ("dp", "seq"), axis=0, tiled=True),
        lax.all_gather(shards[3], ("dp", "seq"), axis=0, tiled=True),
        lax.all_gather(shards[4], ("dp", "seq"), axis=0, tiled=True),
        lax.all_gather(shards[5], ("dp", "seq"), axis=0, tiled=True),
        lax.all_gather(shards[6], ("dp", "seq"), axis=0, tiled=True),
    )
    projected = project(inputs, attention_gain, gathered)
    fetched = (
        lax.all_gather(
            projected[3].reshape(row_count, local_tokens, INNER), "seq", axis=1, tiled=True
        ),
        lax.all_gather(
            projected[4].reshape(row_count, local_tokens, INNER), "seq", axis=1, tiled=True
        ),
    )
    kept_state = forward_rest(
        inputs,
        projected,
        fetched,
        gathered,
        bias_full,
        allowed,
        feedforward_gain,
        delete_gain,
        delete_weight,
        delete_bias,
    )
    block_output = kept_state[8].astype(jnp.bfloat16).reshape(row_count, local_tokens, D)
    delete_gate = (DEPTH * jax.nn.sigmoid(kept_state[11])).reshape(row_count, local_tokens)
    gathered = (
        lax.all_gather(shards[0], ("dp", "seq"), axis=0, tiled=True),
        lax.all_gather(shards[1], ("dp", "seq"), axis=0, tiled=True),
        lax.all_gather(shards[2], ("dp", "seq"), axis=0, tiled=True),
        lax.all_gather(shards[3], ("dp", "seq"), axis=0, tiled=True),
        lax.all_gather(shards[4], ("dp", "seq"), axis=0, tiled=True),
        lax.all_gather(shards[5], ("dp", "seq"), axis=0, tiled=True),
        lax.all_gather(shards[6], ("dp", "seq"), axis=0, tiled=True),
    )
    projected = project(inputs, attention_gain, gathered)
    fetched = (
        lax.all_gather(
            projected[3].reshape(row_count, local_tokens, INNER), "seq", axis=1, tiled=True
        ),
        lax.all_gather(
            projected[4].reshape(row_count, local_tokens, INNER), "seq", axis=1, tiled=True
        ),
    )
    kept_state = forward_rest(
        inputs,
        projected,
        fetched,
        gathered,
        bias_full,
        allowed,
        feedforward_gain,
        delete_gain,
        delete_weight,
        delete_bias,
    )
    (
        probs,
        mixed,
        after_attn,
        scale_two,
        normed_two,
        gate_pre,
        up_pre,
        hidden,
        after_ffn,
        scale_three,
        normed_three,
        logits,
    ) = kept_state
    scale_one, normed_one, query, keys, values = projected
    keys_all, values_all = fetched
    w_query = gathered[0].reshape(D, INNER)
    w_key = gathered[1].reshape(D, INNER)
    w_value = gathered[2].reshape(D, INNER)
    w_out = gathered[3].reshape(INNER, D)
    w_gelu = gathered[4].reshape(D, FF)
    w_up = gathered[5].reshape(D, FF)
    w_down = gathered[6].reshape(FF, D)
    out_cot = output_cotangent.astype(jnp.float32).reshape(-1, D)
    gate_cot = gate_cotangent.reshape(-1)
    sigmoid_vals = jax.nn.sigmoid(logits)
    logit_grad = gate_cot * DEPTH * sigmoid_vals * (1.0 - sigmoid_vals)
    delete_bias_grad = jnp.sum(logit_grad).reshape(1)
    delete_weight_grad = jnp.dot(logit_grad, normed_three, precision=HIGH)
    normed_three_grad = logit_grad[:, None] * delete_weight[None, :]
    delete_gain_grad = jnp.sum(normed_three_grad * after_ffn * scale_three, axis=0)
    resid_two_grad = out_cot + norm_back(after_ffn, scale_three, delete_gain, normed_three_grad)
    branch_grad = resid_two_grad.astype(jnp.bfloat16)
    down_grad = jnp.einsum("nf,nd->fd", hidden, branch_grad, preferred_element_type=jnp.float32)
    hidden_grad = jnp.einsum("nd,fd->nf", branch_grad, w_down, preferred_element_type=jnp.float32)
    gate_grad = (hidden_grad * up_pre * gelu_slope(gate_pre)).astype(jnp.bfloat16)
    up_grad = (hidden_grad * gelu_tanh(gate_pre)).astype(jnp.bfloat16)
    gelu_grad_w = jnp.einsum("nd,nf->df", normed_two, gate_grad, preferred_element_type=jnp.float32)
    up_grad_w = jnp.einsum("nd,nf->df", normed_two, up_grad, preferred_element_type=jnp.float32)
    normed_two_grad = jnp.einsum("nf,df->nd", gate_grad, w_gelu, preferred_element_type=jnp.float32)
    normed_two_grad = normed_two_grad + jnp.einsum(
        "nf,df->nd", up_grad, w_up, preferred_element_type=jnp.float32
    )
    feedforward_gain_grad = jnp.sum(normed_two_grad * after_attn * scale_two, axis=0)
    resid_one_grad = resid_two_grad + norm_back(
        after_attn, scale_two, feedforward_gain, normed_two_grad
    )
    attn_branch_grad = resid_one_grad.astype(jnp.bfloat16)
    out_grad_w = jnp.einsum(
        "ni,nd->id", mixed, attn_branch_grad, preferred_element_type=jnp.float32
    )
    mixed_grad = jnp.einsum(
        "nd,id->ni", attn_branch_grad, w_out, preferred_element_type=jnp.float32
    ).astype(jnp.bfloat16)
    mixed_four = mixed_grad.reshape(row_count, local_tokens, HEADS, HEAD_DIM)
    query_four = query.reshape(row_count, local_tokens, HEADS, HEAD_DIM)
    keys_four = keys_all.reshape(row_count, seq_length, HEADS, HEAD_DIM)
    values_four = values_all.reshape(row_count, seq_length, HEADS, HEAD_DIM)
    probs_low = probs.astype(jnp.bfloat16)
    probs_grad = jnp.einsum(
        "rqhd,rkhd->rhqk", mixed_four, values_four, preferred_element_type=jnp.float32
    )
    value_terms = jnp.einsum(
        "rhqk,rqhd->rkhd", probs_low, mixed_four, preferred_element_type=jnp.float32
    )
    score_grad = probs * (probs_grad - jnp.sum(probs * probs_grad, axis=-1, keepdims=True))
    score_low = score_grad.astype(jnp.bfloat16)
    query_grad = jnp.einsum(
        "rhqk,rkhd->rqhd", score_low, keys_four, preferred_element_type=jnp.float32
    )
    query_grad = query_grad.astype(jnp.bfloat16).reshape(-1, INNER)
    key_terms = jnp.einsum(
        "rhqk,rqhd->rkhd", score_low, query_four, preferred_element_type=jnp.float32
    )
    key_sum, value_sum = (
        lax.psum_scatter(
            key_terms.reshape(row_count, seq_length, INNER).astype(jnp.bfloat16),
            "seq",
            scatter_dimension=1,
            tiled=True,
        ).astype(jnp.float32),
        lax.psum_scatter(
            value_terms.reshape(row_count, seq_length, INNER).astype(jnp.bfloat16),
            "seq",
            scatter_dimension=1,
            tiled=True,
        ).astype(jnp.float32),
    )
    key_grad = key_sum.astype(jnp.bfloat16).reshape(-1, INNER)
    value_grad = value_sum.astype(jnp.bfloat16).reshape(-1, INNER)
    table_grad = jnp.einsum("hqk,qkb->bh", jnp.sum(score_grad, axis=0), one_hot, precision=HIGH)
    query_grad_w = jnp.einsum(
        "nd,ni->di", normed_one, query_grad, preferred_element_type=jnp.float32
    )
    key_grad_w = jnp.einsum("nd,ni->di", normed_one, key_grad, preferred_element_type=jnp.float32)
    value_grad_w = jnp.einsum(
        "nd,ni->di", normed_one, value_grad, preferred_element_type=jnp.float32
    )
    normed_one_grad = jnp.einsum(
        "ni,di->nd", query_grad, w_query, preferred_element_type=jnp.float32
    )
    normed_one_grad = normed_one_grad + jnp.einsum(
        "ni,di->nd", key_grad, w_key, preferred_element_type=jnp.float32
    )
    normed_one_grad = normed_one_grad + jnp.einsum(
        "ni,di->nd", value_grad, w_value, preferred_element_type=jnp.float32
    )
    attention_gain_grad = jnp.sum(normed_one_grad * inputs * scale_one, axis=0)
    input_gradient = (
        resid_one_grad + norm_back(inputs, scale_one, attention_gain, normed_one_grad)
    ).reshape(row_count, local_tokens, D)
    partials = (
        query_grad_w.reshape(-1),
        key_grad_w.reshape(-1),
        value_grad_w.reshape(-1),
        out_grad_w.reshape(-1),
        gelu_grad_w.reshape(-1),
        up_grad_w.reshape(-1),
        down_grad.reshape(-1),
    )
    owned = (
        lax.psum_scatter(partials[0], ("dp", "seq"), scatter_dimension=0, tiled=True),
        lax.psum_scatter(partials[1], ("dp", "seq"), scatter_dimension=0, tiled=True),
        lax.psum_scatter(partials[2], ("dp", "seq"), scatter_dimension=0, tiled=True),
        lax.psum_scatter(partials[3], ("dp", "seq"), scatter_dimension=0, tiled=True),
        lax.psum_scatter(partials[4], ("dp", "seq"), scatter_dimension=0, tiled=True),
        lax.psum_scatter(partials[5], ("dp", "seq"), scatter_dimension=0, tiled=True),
        lax.psum_scatter(partials[6], ("dp", "seq"), scatter_dimension=0, tiled=True),
    )
    summed = lax.psum(
        (
            attention_gain_grad,
            table_grad,
            feedforward_gain_grad,
            delete_gain_grad,
            delete_weight_grad,
            delete_bias_grad,
        ),
        ("dp", "seq"),
    )
    return (
        block_output,
        delete_gate,
        input_gradient,
        summed[0],
        owned[0],
        owned[1],
        owned[2],
        owned[3],
        summed[1],
        summed[2],
        owned[4],
        owned[5],
        owned[6],
        summed[3],
        summed[4],
        summed[5],
    )


class Links:
    def __init__(self, send_sems, recv_sems):
        self.send_sems = send_sems
        self.recv_sems = recv_sems
        self.count = 0
        self.names = {}
        self.sent = []
        self.dp = lax.axis_index("dp")
        self.seq = lax.axis_index("seq")
        self.z = self.dp // 2
        self.x = self.dp % 2
        self.y = self.seq // 2
        self.core = self.seq % 2

    def at(self, z, x):
        return z * 2 + x

    def peer(self, kind):
        if kind == "up":
            return (self.dp + 2, self.seq)
        if kind == "down":
            return (self.dp - 2, self.seq)
        if kind == "x":
            return (self.z * 2 + 1 - self.x, self.seq)
        if kind == "y":
            return (self.dp, (1 - self.y) * 2 + self.core)
        if kind == "core":
            return (self.dp, self.y * 2 + 1 - self.core)
        return (self.dp, (1 - self.y) * 2 + 1 - self.core)

    def copy(self, name, src, dst, kind):
        if name not in self.names:
            self.names[name] = self.count
            self.count += 1
        slot = self.names[name]
        return pltpu.make_async_remote_copy(
            src_ref=src,
            dst_ref=dst,
            send_sem=self.send_sems.at[slot],
            recv_sem=self.recv_sems.at[slot],
            device_id=self.peer(kind),
            device_id_type=pl.DeviceIdType.MESH,
        )

    def greet(self, seq_peers=("y", "core", "diag")):
        barrier = pltpu.get_barrier_semaphore()
        for kind in ("x",) + seq_peers:
            pl.semaphore_signal(
                barrier, inc=1, device_id=self.peer(kind), device_id_type=pl.DeviceIdType.MESH
            )

        @pl.when(self.z < 3)
        def _():
            pl.semaphore_signal(
                barrier, inc=1, device_id=self.peer("up"), device_id_type=pl.DeviceIdType.MESH
            )

        @pl.when(self.z > 0)
        def _():
            pl.semaphore_signal(
                barrier, inc=1, device_id=self.peer("down"), device_id_type=pl.DeviceIdType.MESH
            )

        ends = jnp.where(self.z < 3, 1, 0) + jnp.where(self.z > 0, 1, 0)
        pl.semaphore_wait(barrier, 1 + len(seq_peers) + ends)


def gather_kernel(
    a01, a2, aqkv, awo, o01, o2, oqkv, owo, mine01, send_sems, recv_sems
):
    net = Links(send_sems, recv_sems)
    dp, seq, z, x = net.dp, net.seq, net.z, net.x
    net.greet()
    pending = []

    def send(name, src, dst, kind, when=None):
        if when is None:
            made = net.copy(name, src, dst, kind)
            made.start()
        else:

            @pl.when(when)
            def _():
                net.copy(name, src, dst, kind).start()

        pending.append((name, src, dst, kind, when))

    def wait(name, dst, kind, when=None):
        def now():
            net.copy(name, dst, dst, kind).wait_recv()

        if when is None:
            now()
        else:
            pl.when(when)(now)

    for kind, slot in (
        ("core", net.y * 2 + 1 - net.core),
        ("y", (1 - net.y) * 2 + net.core),
        ("diag", (1 - net.y) * 2 + 1 - net.core),
    ):
        send(("a2a", kind), a01.at[slot], mine01.at[seq], kind)
    mine01[seq] = a01[seq]

    small = (("qkv", aqkv, oqkv), ("wo", awo, owo))
    for name, own, out in small:
        for kind, when in (("up", z < 3), ("down", z > 0), ("x", None), ("y", None), ("core", None)):
            send((name, kind, 0), own, out.at[dp, seq], kind, when)
        out[dp, seq] = own[...]
    for hop in (1, 2, 3):
        for name, _, out in small:
            for way, sign, here, go in (
                ("up", -1, z >= hop, z < 3),
                ("down", 1, z + hop <= 3, z > 0),
            ):
                block = out.at[jnp.clip(dp + 2 * sign * hop, 0, 7), seq]
                wait((name, way, hop - 1), block, way, here)
                if hop < 3:
                    send((name, way, hop), block, block, way, jnp.logical_and(here, go))
                for kind in ("x", "y", "core"):
                    send((name, kind, way, hop), block, block, kind, here)

    for kind, slot in (
        ("core", net.y * 2 + 1 - net.core),
        ("y", (1 - net.y) * 2 + net.core),
        ("diag", (1 - net.y) * 2 + 1 - net.core),
    ):
        wait(("a2a", kind), mine01.at[slot], kind)
    wide = (("w01", mine01, o01), ("w2", a2, o2))
    for name, own, out in wide:
        for kind, when in (("up", z < 3), ("down", z > 0), ("x", None)):
            send((name, kind, 0), own, out.at[dp], kind, when)
        out[dp] = own[...]

    def from_x(hop, way):
        sign = -1 if way == "up" else 1
        here = None if hop == 0 else (z >= hop if way == "up" else z + hop <= 3)
        row = jnp.clip(z + sign * hop, 0, 3)
        return row * 2 + 1 - x, here

    spots = [(0, "up")] + [(h, w) for h in (1, 2, 3) for w in ("up", "down")]
    for hop, way in spots:
        for name, _, out in small:
            where, here = from_x(hop, way)
            tag = (name, "x", 0) if hop == 0 else (name, "x", way, hop)
            block = out.at[where, seq]
            wait(tag, block, "x", here)
            for kind in ("y", "core"):
                send((name, kind, "x", way, hop), block, block, kind, here)
    other_y = (1 - net.y) * 2 + net.core
    for hop, way in spots:
        for name, _, out in small:
            for via in ("own", "x"):
                here = None if hop == 0 else (z >= hop if way == "up" else z + hop <= 3)
                sign = -1 if way == "up" else 1
                row = jnp.clip(z + sign * hop, 0, 3)
                if via == "x":
                    tag = (name, "y", "x", way, hop)
                    where = row * 2 + 1 - x
                elif hop == 0:
                    tag = (name, "y", 0)
                    where = dp
                else:
                    tag = (name, "y", way, hop)
                    where = row * 2 + x
                block = out.at[where, other_y]
                wait(tag, block, "y", here)
                send((name, "relay", via, way, hop), block, block, "core", here)
    for hop in (1, 2, 3):
        for name, _, out in wide:
            for way, sign, here, go in (
                ("up", -1, z >= hop, z < 3),
                ("down", 1, z + hop <= 3, z > 0),
            ):
                block = out.at[jnp.clip(dp + 2 * sign * hop, 0, 7)]
                wait((name, way, hop - 1), block, way, here)
                if hop < 3:
                    send((name, way, hop), block, block, way, jnp.logical_and(here, go))
                send((name, "x", way, hop), block, block, "x", here)
    for hop, way in spots:
        for name, _, out in wide:
            where, here = from_x(hop, way)
            tag = (name, "x", 0) if hop == 0 else (name, "x", way, hop)
            wait(tag, out.at[where], "x", here)
    mate = net.y * 2 + 1 - net.core
    far = (1 - net.y) * 2 + 1 - net.core
    for hop, way in spots:
        for name, _, out in small:
            here = None if hop == 0 else (z >= hop if way == "up" else z + hop <= 3)
            sign = -1 if way == "up" else 1
            row = jnp.clip(z + sign * hop, 0, 3)
            tag = (name, "core", 0) if hop == 0 else (name, "core", way, hop)
            wait(tag, out.at[row * 2 + x, mate], "core", here)
            wait((name, "core", "x", way, hop), out.at[row * 2 + 1 - x, mate], "core", here)
            wait((name, "relay", "own", way, hop), out.at[row * 2 + x, far], "core", here)
            wait((name, "relay", "x", way, hop), out.at[row * 2 + 1 - x, far], "core", here)
    for name, src, dst, kind, when in pending:

        def done(name=name, src=src, dst=dst, kind=kind):
            net.copy(name, src, dst, kind).wait_send()

        if when is None:
            done()
        else:
            pl.when(when)(done)


def gather_all(a01, a2, aqkv, awo):
    here = pl.BlockSpec(memory_space=pltpu.VMEM)
    low = jnp.bfloat16
    return pl.pallas_call(
        gather_kernel,
        out_shape=(
            jax.ShapeDtypeStruct((8,) + a01.shape, low),
            jax.ShapeDtypeStruct((8,) + a2.shape, low),
            jax.ShapeDtypeStruct((8, 4) + aqkv.shape, low),
            jax.ShapeDtypeStruct((8, 4) + awo.shape, low),
        ),
        in_specs=[here] * 4,
        out_specs=(here,) * 4,
        scratch_shapes=[
            pltpu.VMEM(a01.shape, low),
            pltpu.SemaphoreType.DMA((160,)),
            pltpu.SemaphoreType.DMA((160,)),
        ],
        compiler_params=pltpu.CompilerParams(
            collective_id=0, has_side_effects=True, vmem_limit_bytes=50 << 20
        ),
        name="gather_all",
    )(a01, a2, aqkv, awo)


def scatter_kernel(
    g01, g2, gqkv, gwo, r01, r2, rqkv, rwo,
    x01, x2, u01, u2, d01, d2,
    cqkv, cwo, yqkv, ywo, xqkv, xwo, uqkv, uwo, dqkv, dwo,
    send_sems, recv_sems,
):
    net = Links(send_sems, recv_sems)
    dp, seq, z, x = net.dp, net.seq, net.z, net.x
    net.greet()
    pending = []

    def send(name, src, dst, kind, when=None):
        def go():
            net.copy(name, src, dst, kind).start()

        if when is None:
            go()
        else:
            pl.when(when)(go)
        pending.append((name, src, dst, kind, when))

    def wait(name, dst, kind):
        net.copy(name, dst, dst, kind).wait_recv()

    def add(to, plus):
        lead = to.shape[0] if len(to.shape) == 3 else 0
        if lead:
            for i in range(lead):
                to[i] = (to[i].astype(jnp.float32) + plus[i].astype(jnp.float32)).astype(to.dtype)
        else:
            to[...] = (to[...].astype(jnp.float32) + plus[...].astype(jnp.float32)).astype(to.dtype)

    spots = [(h, w) for h in (3, 2, 1) for w in ("up", "down")] + [(0, "up")]

    def target(hop, way):
        sign = 1 if way == "up" else -1
        here = None if hop == 0 else (z + hop <= 3 if way == "up" else z >= hop)
        return jnp.clip(z + sign * hop, 0, 3), here

    wide = (("w01", g01, x01, u01, d01), ("w2", g2, x2, u2, d2))
    narrow = (
        ("qkv", gqkv, cqkv, yqkv, xqkv, uqkv, dqkv),
        ("wo", gwo, cwo, ywo, xwo, uwo, dwo),
    )
    for hop, way in spots:
        row, here = target(hop, way)
        for name, own, xin, _, _ in wide:
            send((name, "x", way, hop), own.at[row * 2 + 1 - x], xin.at[row], "x", here)
    mate = 1 - net.core
    for name, own, cin, _, _, _, _ in narrow:
        for dpi in range(8):
            for yy in range(2):
                send(
                    (name, "core", dpi, yy),
                    own.at[dpi, yy * 2 + mate],
                    cin.at[dpi, yy],
                    "core",
                )
    for name, own, cin, yin, _, _, _ in narrow:
        for dpi in range(8):
            for yy in range(2):
                wait((name, "core", dpi, yy), cin.at[dpi, yy], "core")
                add(cin.at[dpi, yy], own.at[dpi, yy * 2 + net.core])
        for dpi in range(8):
            send(
                (name, "y", dpi),
                cin.at[dpi, 1 - net.y],
                yin.at[dpi],
                "y",
            )

    def along_z(name, own, xin, uin, din, index):
        for hop, way in spots:
            row, here = target(hop, way)

            def step(name=name, hop=hop, way=way, row=row):
                block = xin.at[row]
                wait((name, "x", way, hop), block, "x")
                add(block, own.at[index(row, x)])
                if hop == 0:
                    for other, came in (("up", z > 0), ("down", z < 3)):
                        kept = uin if other == "up" else din

                        @pl.when(came)
                        def _(other=other, kept=kept):
                            wait((name, other, 1), kept.at[z], other)
                            add(block, kept.at[z])

                else:
                    kept = uin if way == "up" else din
                    came = z > 0 if way == "up" else z < 3
                    if hop < 3:

                        @pl.when(came)
                        def _():
                            wait((name, way, hop + 1), kept.at[row], way)
                            add(block, kept.at[row])

            if here is None:
                step()
            else:
                pl.when(here)(step)
            if hop:
                kept = uin if way == "up" else din
                send((name, way, hop), xin.at[row], kept.at[row], way, here)

    for name, own, xin, uin, din in wide:
        along_z(name, own, xin, uin, din, lambda row, col: row * 2 + col)
    for kind, slot in (
        ("core", net.y * 2 + 1 - net.core),
        ("y", (1 - net.y) * 2 + net.core),
        ("diag", (1 - net.y) * 2 + 1 - net.core),
    ):
        send(("a2a", kind), x01.at[z, slot], r01.at[seq], kind)
    r01[seq] = x01[z, seq]
    r2[...] = x2[z]
    for name, own, cin, yin, xin, uin, din in narrow:
        for dpi in range(8):
            wait((name, "y", dpi), yin.at[dpi], "y")
            add(cin.at[dpi, net.y], yin.at[dpi])
        for hop, way in spots:
            row, here = target(hop, way)
            send((name, "x", way, hop), cin.at[row * 2 + 1 - x, net.y], xin.at[row], "x", here)
    for name, own, cin, yin, xin, uin, din in narrow:

        def index(row, col):
            return (row * 2 + col, net.y)

        along_z(name, cin, xin, uin, din, index)
    rqkv[...] = xqkv[z]
    rwo[...] = xwo[z]
    for kind, slot in (
        ("core", net.y * 2 + 1 - net.core),
        ("y", (1 - net.y) * 2 + net.core),
        ("diag", (1 - net.y) * 2 + 1 - net.core),
    ):
        wait(("a2a", kind), r01.at[slot], kind)
    for name, src, dst, kind, when in pending:

        def done(name=name, src=src, dst=dst, kind=kind):
            net.copy(name, src, dst, kind).wait_send()

        if when is None:
            done()
        else:
            pl.when(when)(done)


def scatter_all(g01, g2, gqkv, gwo):
    here = pl.BlockSpec(memory_space=pltpu.VMEM)
    low = jnp.bfloat16
    shapes = (g01.shape[1:], g2.shape[1:], gqkv.shape[2:], gwo.shape[2:])
    fours = [pltpu.VMEM((4,) + s, low) for s in shapes]
    return pl.pallas_call(
        scatter_kernel,
        out_shape=tuple(jax.ShapeDtypeStruct(s, low) for s in shapes),
        in_specs=[here] * 4,
        out_specs=(here,) * 4,
        scratch_shapes=[
            fours[0], fours[1], fours[0], fours[1], fours[0], fours[1],
            pltpu.VMEM((8, 2) + shapes[2], low), pltpu.VMEM((8, 2) + shapes[3], low),
            pltpu.VMEM((8,) + shapes[2], low), pltpu.VMEM((8,) + shapes[3], low),
            fours[2], fours[3], fours[2], fours[3], fours[2], fours[3],
            pltpu.SemaphoreType.DMA((160,)),
            pltpu.SemaphoreType.DMA((160,)),
        ],
        compiler_params=pltpu.CompilerParams(
            collective_id=1, has_side_effects=True, vmem_limit_bytes=60 << 20
        ),
        name="scatter_all",
    )(g01, g2, gqkv, gwo)


def local_rows(
    block_input, segment_ids, attention_gain, query_weight, key_weight, value_weight,
    output_weight, bias_table, feedforward_gain, gelu_weight, up_weight, down_weight,
    delete_gain, delete_weight, delete_bias, output_cotangent, gate_cotangent,
):
    low, full = jnp.bfloat16, jnp.float32
    seq_length = segment_ids.shape[1]
    tokens = block_input.shape[1]
    offset = lax.axis_index("seq") * tokens
    inputs = block_input.astype(full).reshape(tokens, D)
    half = FF // 4

    def by_column(flat):
        return flat.reshape(46, 8, 4, 112).transpose(2, 0, 1, 3).reshape(4, 46, half)

    a01 = jnp.concatenate([by_column(gelu_weight), by_column(up_weight)], axis=2)
    aqkv = jnp.concatenate(
        [w.reshape(46, INNER) for w in (query_weight, key_weight, value_weight)], axis=1
    )
    o01, o2, oqkv, owo = gather_all(
        a01, down_weight.reshape(112, D), aqkv, output_weight.reshape(12, D)
    )
    w01 = o01.reshape(D, 2 * half)
    w2 = o2.reshape(half, D)
    wqkv = oqkv.reshape(D, 3 * INNER)
    wo = owo.reshape(INNER, D)

    def dot(a, b):
        return jnp.dot(a, b, preferred_element_type=full)

    def dot_nt(a, b):
        return lax.dot_general(a, b, (((1,), (1,)), ((), ())), preferred_element_type=full)

    def dot_tn(a, b):
        return lax.dot_general(a, b, (((0,), (0,)), ((), ())), preferred_element_type=full)

    scale_one = norm_scale(inputs)
    normed_one = (inputs * scale_one * attention_gain).astype(low)
    qkv = dot(normed_one, wqkv).astype(low)
    query = qkv[:, :INNER]
    kv_all = lax.all_gather(qkv[:, INNER:], "seq", axis=0, tiled=True)

    grid_all = jnp.asarray(bucket_grid(seq_length, BUCKETS, MAX_DIST))
    local_buckets = lax.dynamic_slice_in_dim(grid_all, offset, tokens, 0)
    one_hot = (local_buckets[:, :, None] == lax.iota(jnp.int32, BUCKETS)[None, None, :]).astype(full)
    bias_full = jnp.einsum("qkb,bh->hqk", one_hot, bias_table, precision=HIGH)
    query_docs = lax.dynamic_slice_in_dim(segment_ids, offset, tokens, 1)[0]
    allowed = query_docs[:, None] == segment_ids[0][None, :]
    q4 = query.reshape(tokens, HEADS, HEAD_DIM)
    k4 = kv_all[:, :INNER].reshape(seq_length, HEADS, HEAD_DIM)
    v4 = kv_all[:, INNER:].reshape(seq_length, HEADS, HEAD_DIM)
    scores = jnp.einsum("qhd,khd->hqk", q4, k4, preferred_element_type=full) + bias_full
    scores = jnp.where(allowed[None], scores, -1e30)
    expo = jnp.exp(scores - jnp.max(scores, axis=-1, keepdims=True))
    probs = expo / jnp.sum(expo, axis=-1, keepdims=True)
    mixed = jnp.einsum("hqk,khd->qhd", probs.astype(low), v4, preferred_element_type=full)
    mixed = mixed.astype(low).reshape(tokens, INNER)
    after_attn = inputs + dot(mixed, wo)
    scale_two = norm_scale(after_attn)
    normed_two = (after_attn * scale_two * feedforward_gain).astype(low)
    n2_all = lax.all_gather(normed_two, "seq", axis=0, tiled=True)
    pre = dot(n2_all, w01)
    gate_pre, up_pre = pre[:, :half], pre[:, half:]
    hidden = (gelu_tanh(gate_pre) * up_pre).astype(low)
    ffn = lax.psum_scatter(dot(hidden, w2).astype(low), "seq", scatter_dimension=0, tiled=True)
    after_ffn = after_attn + ffn.astype(full)
    scale_three = norm_scale(after_ffn)
    normed_three = after_ffn * scale_three * delete_gain
    logits = jnp.sum(normed_three * delete_weight, axis=-1) + delete_bias[0]
    block_output = after_ffn.astype(low).reshape(1, tokens, D)
    sigmoid_vals = jax.nn.sigmoid(logits)
    delete_gate = (DEPTH * sigmoid_vals).reshape(1, tokens)

    out_cot = output_cotangent.astype(full).reshape(tokens, D)
    logit_grad = gate_cotangent.reshape(-1) * DEPTH * sigmoid_vals * (1.0 - sigmoid_vals)
    delete_bias_grad = jnp.sum(logit_grad).reshape(1)
    delete_weight_grad = jnp.sum(logit_grad[:, None] * normed_three, axis=0)
    normed_three_grad = logit_grad[:, None] * delete_weight[None, :]
    delete_gain_grad = jnp.sum(normed_three_grad * after_ffn * scale_three, axis=0)
    resid_two_grad = out_cot + norm_back(after_ffn, scale_three, delete_gain, normed_three_grad)
    branch_all = lax.all_gather(resid_two_grad.astype(low), "seq", axis=0, tiled=True)
    g2 = dot_tn(hidden, branch_all).astype(low).reshape(8, 112, D)
    hidden_grad = dot_nt(branch_all, w2)
    gate_grad = (hidden_grad * up_pre * gelu_slope(gate_pre)).astype(low)
    up_grad = (hidden_grad * gelu_tanh(gate_pre)).astype(low)
    both = jnp.concatenate([gate_grad, up_grad], axis=1)
    g01 = dot_tn(n2_all, both).astype(low).reshape(8, 4, 46, 2 * half)
    normed_two_grad = lax.psum_scatter(
        dot_nt(both, w01).astype(low), "seq", scatter_dimension=0, tiled=True
    ).astype(full)
    feedforward_gain_grad = jnp.sum(normed_two_grad * after_attn * scale_two, axis=0)
    resid_one_grad = resid_two_grad + norm_back(
        after_attn, scale_two, feedforward_gain, normed_two_grad
    )
    attn_branch = resid_one_grad.astype(low)
    gwo = dot_tn(mixed, attn_branch).astype(low).reshape(8, 4, 12, D)
    mixed_grad = dot_nt(attn_branch, wo).astype(low)
    m4 = mixed_grad.reshape(tokens, HEADS, HEAD_DIM)
    probs_grad = jnp.einsum("qhd,khd->hqk", m4, v4, preferred_element_type=full)
    value_terms = jnp.einsum("hqk,qhd->khd", probs.astype(low), m4, preferred_element_type=full)
    score_grad = probs * (probs_grad - jnp.sum(probs * probs_grad, axis=-1, keepdims=True))
    score_low = score_grad.astype(low)
    query_grad = jnp.einsum("hqk,khd->qhd", score_low, k4, preferred_element_type=full)
    query_grad = query_grad.astype(low).reshape(tokens, INNER)
    key_terms = jnp.einsum("hqk,qhd->khd", score_low, q4, preferred_element_type=full)
    kv_terms = jnp.concatenate(
        [key_terms.reshape(seq_length, INNER), value_terms.reshape(seq_length, INNER)], axis=1
    ).astype(low)
    kv_grad = lax.psum_scatter(kv_terms, "seq", scatter_dimension=0, tiled=True)
    table_grad = jnp.einsum("hqk,qkb->bh", score_grad, one_hot, precision=HIGH)
    qkv_grad = jnp.concatenate([query_grad, kv_grad], axis=1)
    gqkv = dot_tn(normed_one, qkv_grad).astype(low).reshape(8, 4, 46, 3 * INNER)
    normed_one_grad = dot_nt(qkv_grad, wqkv)
    attention_gain_grad = jnp.sum(normed_one_grad * inputs * scale_one, axis=0)
    input_gradient = (
        resid_one_grad + norm_back(inputs, scale_one, attention_gain, normed_one_grad)
    ).reshape(1, tokens, D)
    r01, r2, rqkv, rwo = scatter_all(g01, g2, gqkv, gwo)

    def by_row(cols):
        return (
            cols.astype(full).reshape(4, 46, 8, 112).transpose(1, 2, 0, 3).reshape(46 * FF)
        )

    summed = lax.psum(
        (
            attention_gain_grad,
            table_grad,
            feedforward_gain_grad,
            delete_gain_grad,
            delete_weight_grad,
            delete_bias_grad,
        ),
        ("dp", "seq"),
    )
    narrow = rqkv.astype(full)
    return (
        block_output,
        delete_gate,
        input_gradient,
        summed[0],
        narrow[:, :INNER].reshape(-1),
        narrow[:, INNER : 2 * INNER].reshape(-1),
        narrow[:, 2 * INNER :].reshape(-1),
        rwo.astype(full).reshape(-1),
        summed[1],
        summed[2],
        by_row(r01[:, :, :half]),
        by_row(r01[:, :, half:]),
        r2.astype(full).reshape(-1),
        summed[3],
        summed[4],
        summed[5],
    )


def solution(mesh):
    placed = (
        P("dp", "seq", None),
        P("dp", None),
        P(),
        P(("dp", "seq")),
        P(("dp", "seq")),
        P(("dp", "seq")),
        P(("dp", "seq")),
        P(),
        P(),
        P(("dp", "seq")),
        P(("dp", "seq")),
        P(("dp", "seq")),
        P(),
        P(),
        P(),
        P("dp", "seq", None),
        P("dp", "seq"),
    )
    fast = mesh.shape["dp"] == 8 and mesh.shape["seq"] == 4
    return jax.shard_map(
        local_rows if fast else local,
        mesh=mesh,
        in_specs=placed,
        out_specs=(
            P("dp", "seq", None),
            P("dp", "seq"),
            P("dp", "seq", None),
            P(),
            P(("dp", "seq")),
            P(("dp", "seq")),
            P(("dp", "seq")),
            P(("dp", "seq")),
            P(),
            P(),
            P(("dp", "seq")),
            P(("dp", "seq")),
            P(("dp", "seq")),
            P(),
            P(),
            P(),
        ),
        check_vma=False,
    )
```

```python
import math

import jax
import jax.numpy as jnp
import numpy as np
from jax import lax
from jax.experimental import pallas as pl
from jax.experimental.pallas import tpu as pltpu
from jax.sharding import PartitionSpec as P

D = 1472
HEADS = 6
HEAD_DIM = 64
FF = 3584
BUCKETS = 32
MAX_DIST = 128
INNER = 384


EPS = 1e-06
HIGH = lax.Precision.HIGHEST
SLOPE = 0.7978845608028654
CUBIC = 0.044715
DEPTH = -30.0


def relative_buckets(length, buckets, reach):
    half = buckets // 2
    exact = half // 2
    offsets = np.arange(-(length - 1), length)
    distance = np.abs(offsets)
    safe_far = np.maximum(distance, 1)
    spread = exact + np.floor(
        np.log(safe_far / exact) / math.log(reach / exact) * (half - exact)
    ).astype(np.int32)
    spread = np.minimum(spread, half - 1)
    chosen = np.where(distance < exact, distance, spread) + np.where(offsets > 0, half, 0)
    return chosen.astype(np.int32)


def bucket_grid(length, buckets, reach):
    flat = relative_buckets(length, buckets, reach)
    places = np.arange(length)
    return flat[places[None, :] - places[:, None] + length - 1].astype(np.int32)


def gelu_tanh(value):
    return 0.5 * value * (1.0 + jnp.tanh(SLOPE * (value + CUBIC * value * value * value)))


def gelu_slope(value):
    tangent = jnp.tanh(SLOPE * (value + CUBIC * value * value * value))
    return 0.5 * (1.0 + tangent) + 0.5 * value * (1.0 - tangent * tangent) * SLOPE * (
        1.0 + 3.0 * CUBIC * value * value
    )


def norm_scale(value):
    return lax.rsqrt(jnp.mean(value * value, axis=-1, keepdims=True) + EPS)


def norm_back(value, scaling, gain, upstream):
    weighted = gain * upstream
    return scaling * weighted - value * (scaling * scaling * scaling) * jnp.mean(
        value * weighted, axis=-1, keepdims=True
    )


def project(inputs, gain, gathered):
    scale_one = norm_scale(inputs)
    normed_one = (inputs * scale_one * gain).astype(jnp.bfloat16)
    query = jnp.dot(
        normed_one, gathered[0].reshape(D, INNER), preferred_element_type=jnp.float32
    ).astype(jnp.bfloat16)
    keys = jnp.dot(
        normed_one, gathered[1].reshape(D, INNER), preferred_element_type=jnp.float32
    ).astype(jnp.bfloat16)
    values = jnp.dot(
        normed_one, gathered[2].reshape(D, INNER), preferred_element_type=jnp.float32
    ).astype(jnp.bfloat16)
    return (scale_one, normed_one, query, keys, values)


def forward_rest(
    inputs,
    projected,
    fetched,
    gathered,
    bias_full,
    allowed,
    feedforward_gain,
    delete_gain,
    delete_weight,
    delete_bias,
):
    query = projected[2]
    keys_all, values_all = fetched
    row_count = keys_all.shape[0]
    query_four = query.reshape(row_count, -1, HEADS, HEAD_DIM)
    keys_four = keys_all.reshape(row_count, -1, HEADS, HEAD_DIM)
    values_four = values_all.reshape(row_count, -1, HEADS, HEAD_DIM)
    scores = (
        jnp.einsum("rqhd,rkhd->rhqk", query_four, keys_four, preferred_element_type=jnp.float32)
        + bias_full[None]
    )
    scores = jnp.where(allowed, scores, -1e30)
    peak = jnp.max(scores, axis=-1, keepdims=True)
    expo = jnp.exp(scores - peak)
    probs = expo / jnp.sum(expo, axis=-1, keepdims=True)
    mixed = jnp.einsum(
        "rhqk,rkhd->rqhd",
        probs.astype(jnp.bfloat16),
        values_four,
        preferred_element_type=jnp.float32,
    )
    mixed = mixed.astype(jnp.bfloat16).reshape(-1, INNER)
    after_attn = inputs + jnp.dot(
        mixed, gathered[3].reshape(INNER, D), preferred_element_type=jnp.float32
    )
    scale_two = norm_scale(after_attn)
    normed_two = (after_attn * scale_two * feedforward_gain).astype(jnp.bfloat16)
    gate_pre = jnp.dot(normed_two, gathered[4].reshape(D, FF), preferred_element_type=jnp.float32)
    up_pre = jnp.dot(normed_two, gathered[5].reshape(D, FF), preferred_element_type=jnp.float32)
    hidden = (gelu_tanh(gate_pre) * up_pre).astype(jnp.bfloat16)
    after_ffn = after_attn + jnp.dot(
        hidden, gathered[6].reshape(FF, D), preferred_element_type=jnp.float32
    )
    scale_three = norm_scale(after_ffn)
    normed_three = after_ffn * scale_three * delete_gain
    logits = jnp.dot(normed_three, delete_weight, precision=HIGH) + delete_bias[0]
    return (
        probs,
        mixed,
        after_attn,
        scale_two,
        normed_two,
        gate_pre,
        up_pre,
        hidden,
        after_ffn,
        scale_three,
        normed_three,
        logits,
    )


def local(
    block_input,
    segment_ids,
    attention_gain,
    query_weight,
    key_weight,
    value_weight,
    output_weight,
    bias_table,
    feedforward_gain,
    gelu_weight,
    up_weight,
    down_weight,
    delete_gain,
    delete_weight,
    delete_bias,
    output_cotangent,
    gate_cotangent,
):
    row_count = block_input.shape[0]
    local_tokens = block_input.shape[1]
    seq_length = segment_ids.shape[1]
    offset = lax.axis_index("seq") * local_tokens
    inputs = block_input.astype(jnp.float32).reshape(-1, D)
    grid_all = jnp.asarray(bucket_grid(seq_length, BUCKETS, MAX_DIST))
    local_buckets = lax.dynamic_slice_in_dim(grid_all, offset, local_tokens, 0)
    one_hot = (local_buckets[:, :, None] == lax.iota(jnp.int32, BUCKETS)[None, None, :]).astype(
        jnp.float32
    )
    bias_full = jnp.einsum("qkb,bh->hqk", one_hot, bias_table, precision=HIGH)
    query_docs = lax.dynamic_slice_in_dim(segment_ids, offset, local_tokens, 1)
    allowed = (query_docs[:, :, None] == segment_ids[:, None, :])[:, None]
    shards = (
        query_weight,
        key_weight,
        value_weight,
        output_weight,
        gelu_weight,
        up_weight,
        down_weight,
    )
    gathered = (
        lax.all_gather(shards[0], ("dp", "seq"), axis=0, tiled=True),
        lax.all_gather(shards[1], ("dp", "seq"), axis=0, tiled=True),
        lax.all_gather(shards[2], ("dp", "seq"), axis=0, tiled=True),
        lax.all_gather(shards[3], ("dp", "seq"), axis=0, tiled=True),
        lax.all_gather(shards[4], ("dp", "seq"), axis=0, tiled=True),
        lax.all_gather(shards[5], ("dp", "seq"), axis=0, tiled=True),
        lax.all_gather(shards[6], ("dp", "seq"), axis=0, tiled=True),
    )
    projected = project(inputs, attention_gain, gathered)
    fetched = (
        lax.all_gather(
            projected[3].reshape(row_count, local_tokens, INNER), "seq", axis=1, tiled=True
        ),
        lax.all_gather(
            projected[4].reshape(row_count, local_tokens, INNER), "seq", axis=1, tiled=True
        ),
    )
    kept_state = forward_rest(
        inputs,
        projected,
        fetched,
        gathered,
        bias_full,
        allowed,
        feedforward_gain,
        delete_gain,
        delete_weight,
        delete_bias,
    )
    block_output = kept_state[8].astype(jnp.bfloat16).reshape(row_count, local_tokens, D)
    delete_gate = (DEPTH * jax.nn.sigmoid(kept_state[11])).reshape(row_count, local_tokens)
    gathered = (
        lax.all_gather(shards[0], ("dp", "seq"), axis=0, tiled=True),
        lax.all_gather(shards[1], ("dp", "seq"), axis=0, tiled=True),
        lax.all_gather(shards[2], ("dp", "seq"), axis=0, tiled=True),
        lax.all_gather(shards[3], ("dp", "seq"), axis=0, tiled=True),
        lax.all_gather(shards[4], ("dp", "seq"), axis=0, tiled=True),
        lax.all_gather(shards[5], ("dp", "seq"), axis=0, tiled=True),
        lax.all_gather(shards[6], ("dp", "seq"), axis=0, tiled=True),
    )
    projected = project(inputs, attention_gain, gathered)
    fetched = (
        lax.all_gather(
            projected[3].reshape(row_count, local_tokens, INNER), "seq", axis=1, tiled=True
        ),
        lax.all_gather(
            projected[4].reshape(row_count, local_tokens, INNER), "seq", axis=1, tiled=True
        ),
    )
    kept_state = forward_rest(
        inputs,
        projected,
        fetched,
        gathered,
        bias_full,
        allowed,
        feedforward_gain,
        delete_gain,
        delete_weight,
        delete_bias,
    )
    (
        probs,
        mixed,
        after_attn,
        scale_two,
        normed_two,
        gate_pre,
        up_pre,
        hidden,
        after_ffn,
        scale_three,
        normed_three,
        logits,
    ) = kept_state
    scale_one, normed_one, query, keys, values = projected
    keys_all, values_all = fetched
    w_query = gathered[0].reshape(D, INNER)
    w_key = gathered[1].reshape(D, INNER)
    w_value = gathered[2].reshape(D, INNER)
    w_out = gathered[3].reshape(INNER, D)
    w_gelu = gathered[4].reshape(D, FF)
    w_up = gathered[5].reshape(D, FF)
    w_down = gathered[6].reshape(FF, D)
    out_cot = output_cotangent.astype(jnp.float32).reshape(-1, D)
    gate_cot = gate_cotangent.reshape(-1)
    sigmoid_vals = jax.nn.sigmoid(logits)
    logit_grad = gate_cot * DEPTH * sigmoid_vals * (1.0 - sigmoid_vals)
    delete_bias_grad = jnp.sum(logit_grad).reshape(1)
    delete_weight_grad = jnp.dot(logit_grad, normed_three, precision=HIGH)
    normed_three_grad = logit_grad[:, None] * delete_weight[None, :]
    delete_gain_grad = jnp.sum(normed_three_grad * after_ffn * scale_three, axis=0)
    resid_two_grad = out_cot + norm_back(after_ffn, scale_three, delete_gain, normed_three_grad)
    branch_grad = resid_two_grad.astype(jnp.bfloat16)
    down_grad = jnp.einsum("nf,nd->fd", hidden, branch_grad, preferred_element_type=jnp.float32)
    hidden_grad = jnp.einsum("nd,fd->nf", branch_grad, w_down, preferred_element_type=jnp.float32)
    gate_grad = (hidden_grad * up_pre * gelu_slope(gate_pre)).astype(jnp.bfloat16)
    up_grad = (hidden_grad * gelu_tanh(gate_pre)).astype(jnp.bfloat16)
    gelu_grad_w = jnp.einsum("nd,nf->df", normed_two, gate_grad, preferred_element_type=jnp.float32)
    up_grad_w = jnp.einsum("nd,nf->df", normed_two, up_grad, preferred_element_type=jnp.float32)
    normed_two_grad = jnp.einsum("nf,df->nd", gate_grad, w_gelu, preferred_element_type=jnp.float32)
    normed_two_grad = normed_two_grad + jnp.einsum(
        "nf,df->nd", up_grad, w_up, preferred_element_type=jnp.float32
    )
    feedforward_gain_grad = jnp.sum(normed_two_grad * after_attn * scale_two, axis=0)
    resid_one_grad = resid_two_grad + norm_back(
        after_attn, scale_two, feedforward_gain, normed_two_grad
    )
    attn_branch_grad = resid_one_grad.astype(jnp.bfloat16)
    out_grad_w = jnp.einsum(
        "ni,nd->id", mixed, attn_branch_grad, preferred_element_type=jnp.float32
    )
    mixed_grad = jnp.einsum(
        "nd,id->ni", attn_branch_grad, w_out, preferred_element_type=jnp.float32
    ).astype(jnp.bfloat16)
    mixed_four = mixed_grad.reshape(row_count, local_tokens, HEADS, HEAD_DIM)
    query_four = query.reshape(row_count, local_tokens, HEADS, HEAD_DIM)
    keys_four = keys_all.reshape(row_count, seq_length, HEADS, HEAD_DIM)
    values_four = values_all.reshape(row_count, seq_length, HEADS, HEAD_DIM)
    probs_low = probs.astype(jnp.bfloat16)
    probs_grad = jnp.einsum(
        "rqhd,rkhd->rhqk", mixed_four, values_four, preferred_element_type=jnp.float32
    )
    value_terms = jnp.einsum(
        "rhqk,rqhd->rkhd", probs_low, mixed_four, preferred_element_type=jnp.float32
    )
    score_grad = probs * (probs_grad - jnp.sum(probs * probs_grad, axis=-1, keepdims=True))
    score_low = score_grad.astype(jnp.bfloat16)
    query_grad = jnp.einsum(
        "rhqk,rkhd->rqhd", score_low, keys_four, preferred_element_type=jnp.float32
    )
    query_grad = query_grad.astype(jnp.bfloat16).reshape(-1, INNER)
    key_terms = jnp.einsum(
        "rhqk,rqhd->rkhd", score_low, query_four, preferred_element_type=jnp.float32
    )
    key_sum, value_sum = (
        lax.psum_scatter(
            key_terms.reshape(row_count, seq_length, INNER).astype(jnp.bfloat16),
            "seq",
            scatter_dimension=1,
            tiled=True,
        ).astype(jnp.float32),
        lax.psum_scatter(
            value_terms.reshape(row_count, seq_length, INNER).astype(jnp.bfloat16),
            "seq",
            scatter_dimension=1,
            tiled=True,
        ).astype(jnp.float32),
    )
    key_grad = key_sum.astype(jnp.bfloat16).reshape(-1, INNER)
    value_grad = value_sum.astype(jnp.bfloat16).reshape(-1, INNER)
    table_grad = jnp.einsum("hqk,qkb->bh", jnp.sum(score_grad, axis=0), one_hot, precision=HIGH)
    query_grad_w = jnp.einsum(
        "nd,ni->di", normed_one, query_grad, preferred_element_type=jnp.float32
    )
    key_grad_w = jnp.einsum("nd,ni->di", normed_one, key_grad, preferred_element_type=jnp.float32)
    value_grad_w = jnp.einsum(
        "nd,ni->di", normed_one, value_grad, preferred_element_type=jnp.float32
    )
    normed_one_grad = jnp.einsum(
        "ni,di->nd", query_grad, w_query, preferred_element_type=jnp.float32
    )
    normed_one_grad = normed_one_grad + jnp.einsum(
        "ni,di->nd", key_grad, w_key, preferred_element_type=jnp.float32
    )
    normed_one_grad = normed_one_grad + jnp.einsum(
        "ni,di->nd", value_grad, w_value, preferred_element_type=jnp.float32
    )
    attention_gain_grad = jnp.sum(normed_one_grad * inputs * scale_one, axis=0)
    input_gradient = (
        resid_one_grad + norm_back(inputs, scale_one, attention_gain, normed_one_grad)
    ).reshape(row_count, local_tokens, D)
    partials = (
        query_grad_w.reshape(-1),
        key_grad_w.reshape(-1),
        value_grad_w.reshape(-1),
        out_grad_w.reshape(-1),
        gelu_grad_w.reshape(-1),
        up_grad_w.reshape(-1),
        down_grad.reshape(-1),
    )
    owned = (
        lax.psum_scatter(partials[0], ("dp", "seq"), scatter_dimension=0, tiled=True),
        lax.psum_scatter(partials[1], ("dp", "seq"), scatter_dimension=0, tiled=True),
        lax.psum_scatter(partials[2], ("dp", "seq"), scatter_dimension=0, tiled=True),
        lax.psum_scatter(partials[3], ("dp", "seq"), scatter_dimension=0, tiled=True),
        lax.psum_scatter(partials[4], ("dp", "seq"), scatter_dimension=0, tiled=True),
        lax.psum_scatter(partials[5], ("dp", "seq"), scatter_dimension=0, tiled=True),
        lax.psum_scatter(partials[6], ("dp", "seq"), scatter_dimension=0, tiled=True),
    )
    summed = lax.psum(
        (
            attention_gain_grad,
            table_grad,
            feedforward_gain_grad,
            delete_gain_grad,
            delete_weight_grad,
            delete_bias_grad,
        ),
        ("dp", "seq"),
    )
    return (
        block_output,
        delete_gate,
        input_gradient,
        summed[0],
        owned[0],
        owned[1],
        owned[2],
        owned[3],
        summed[1],
        summed[2],
        owned[4],
        owned[5],
        owned[6],
        summed[3],
        summed[4],
        summed[5],
    )


class Links:
    def __init__(self, send_sems, recv_sems):
        self.send_sems = send_sems
        self.recv_sems = recv_sems
        self.count = 0
        self.names = {}
        self.sent = []
        self.dp = lax.axis_index("dp")
        self.seq = lax.axis_index("seq")
        self.z = self.dp // 2
        self.x = self.dp % 2
        self.y = self.seq // 2
        self.core = self.seq % 2

    def at(self, z, x):
        return z * 2 + x

    def peer(self, kind):
        if kind == "up":
            return (self.dp + 2, self.seq)
        if kind == "down":
            return (self.dp - 2, self.seq)
        if kind == "z1":
            return (self.dp + 2 - 4 * (self.z % 2), self.seq)
        if kind == "z2":
            return (self.dp + 4 - 8 * (self.z // 2), self.seq)
        if kind == "x":
            return (self.z * 2 + 1 - self.x, self.seq)
        if kind == "y":
            return (self.dp, (1 - self.y) * 2 + self.core)
        if kind == "core":
            return (self.dp, self.y * 2 + 1 - self.core)
        return (self.dp, (1 - self.y) * 2 + 1 - self.core)

    def copy(self, name, src, dst, kind):
        if name not in self.names:
            self.names[name] = self.count
            self.count += 1
        slot = self.names[name]
        return pltpu.make_async_remote_copy(
            src_ref=src,
            dst_ref=dst,
            send_sem=self.send_sems.at[slot],
            recv_sem=self.recv_sems.at[slot],
            device_id=self.peer(kind),
            device_id_type=pl.DeviceIdType.MESH,
        )

    def greet(self, seq_peers, others=(), far=False):
        barrier = pltpu.get_barrier_semaphore()

        def call(kind):
            pl.semaphore_signal(
                barrier, inc=1, device_id=self.peer(kind), device_id_type=pl.DeviceIdType.MESH
            )

        for kind in seq_peers + others:
            call(kind)
        count = len(seq_peers) + len(others)
        if far:
            for kind in ("x", "z2"):
                call(kind)
            pl.when(self.z < 3)(lambda: call("up"))
            pl.when(self.z > 0)(lambda: call("down"))
            count = count + 2 + jnp.where(self.z < 3, 1, 0) + jnp.where(self.z > 0, 1, 0)
        pl.semaphore_wait(barrier, count)


class Mail:
    def __init__(self, net):
        self.net = net
        self.pending = []
        self.local = []

    def send(self, name, src, dst, kind, when=None):
        def go():
            self.net.copy(name, src, dst, kind).start()

        if when is None:
            go()
        else:
            pl.when(when)(go)
        self.pending.append((name, src, dst, kind, when))

    def wait(self, name, dst, kind, when=None):
        def now():
            self.net.copy(name, dst, dst, kind).wait_recv()

        if when is None:
            now()
        else:
            pl.when(when)(now)

    def keep(self, src, dst, sem):
        made = pltpu.make_async_copy(src, dst, sem)
        made.start()
        self.local.append(made)

    def finish(self):
        for name, src, dst, kind, when in self.pending:

            def done(name=name, src=src, dst=dst, kind=kind):
                self.net.copy(name, src, dst, kind).wait_send()

            if when is None:
                done()
            else:
                pl.when(when)(done)
        for made in self.local:
            made.wait()


def dot_nn(a, b):
    return jnp.dot(a, b, preferred_element_type=jnp.float32)


def dot_nt(a, b):
    return lax.dot_general(a, b, (((1,), (1,)), ((), ())), preferred_element_type=jnp.float32)


def dot_tn(a, b):
    return lax.dot_general(a, b, (((0,), (0,)), ((), ())), preferred_element_type=jnp.float32)


def forward_kernel(
    x_in, qdoc, kdoc, window, gain_one, gain_two, a01, a2, aqkv, awo,
    w01_out, w2_out, wqkv_out, wo_out, q_out, kv_out, p_out, mixed_out, h1_out, n2t_out,
    pre_out, hidt_out, h2_out,
    got01, mine01, w01, w2, oqkv, wqkv, owo, wo, probs, query, kv_own, kv_all, mixed,
    h1, n2_own, n2_all, n2_t, pre, hidden, hid_t, fsend, frecv, fysend, fyrecv, h2,
    send_sems, recv_sems, keep_sems,
):
    low, full = jnp.bfloat16, jnp.float32
    net = Links(send_sems, recv_sems)
    mail = Mail(net)
    send, wait = mail.send, mail.wait
    dp, seq, z, x, y, core = net.dp, net.seq, net.z, net.x, net.y, net.core
    s_core, s_y, s_diag = y * 2 + 1 - core, (1 - y) * 2 + core, (1 - y) * 2 + 1 - core
    spots = [(0, "up")] + [(h, w) for h in (1, 2, 3) for w in ("up", "down")]

    def origin(hop, way):
        here = None if hop == 0 else (z >= hop if way == "up" else z + hop <= 3)
        return jnp.clip(z + (-hop if way == "up" else hop), 0, 3), here

    net.greet(("y", "core", "diag"), far=True)
    seats = (("core", s_core), ("y", s_y), ("diag", s_diag))
    for kind, slot in seats:
        send(("a2a", kind), a01.at[slot], got01.at[seq], kind)
    small = (("qkv", aqkv, oqkv), ("wo", awo, owo))
    for name, own, out in small:
        for kind, when in (("y", None), ("up", z < 3), ("down", z > 0), ("x", None), ("core", None)):
            send((name, kind, 0), own, out.at[dp, seq], kind, when)
    got01[seq] = a01[seq]
    for name, own, out in small:
        out[dp, seq] = own[...]

    allowed = qdoc[...] == kdoc[...]

    def bias(head):
        wide = jnp.broadcast_to(window[head : head + 1, :], (256, 1280))
        rolled = pltpu.roll(wide, 0, 1, stride=1, stride_axis=0)[:, 256:1280]
        probs[head] = jnp.where(allowed, rolled, -1e30)

    def small_hop(hop):
        for name, _, out in small:
            for way, go in (("up", z < 3), ("down", z > 0)):
                row, here = origin(hop, way)
                block = out.at[row * 2 + x, seq]
                wait((name, way, hop - 1), block, way, here)
                if hop < 3:
                    send((name, way, hop), block, block, way, jnp.logical_and(here, go))
                for kind in ("y", "x", "core"):
                    send((name, kind, way, hop), block, block, kind, here)

    bias(0)
    small_hop(1)
    bias(1)
    small_hop(2)
    inputs = x_in[...].astype(full)
    scale_one = norm_scale(inputs)
    normed_one = (inputs * scale_one * gain_one[...]).astype(low)
    small_hop(3)

    for kind, slot in seats:
        wait(("a2a", kind), got01.at[slot], kind)
    for s in range(4):
        mine01[46 * s : 46 * s + 46, :] = got01[s]

    def rows01(d):
        return w01.at[pl.ds(pl.multiple_of(d * 184, 8), 184), :]

    def rows2(d):
        return w2.at[pl.ds(pl.multiple_of(d * 112, 8), 112), :]

    wide = {"w01": (mine01, rows01), "w2": (a2, rows2)}
    placed = {}

    def wide_own(name):
        own, rows = wide[name]
        for kind, when in (("up", z < 3), ("down", z > 0), ("x", None)):
            send((name, kind, 0), own, rows(dp), kind, when)
        placed[name] = pltpu.make_async_copy(own, rows(dp), keep_sems.at[0 if name == "w01" else 1])
        placed[name].start()

    def wide_hop(name, hop):
        _, rows = wide[name]
        for way, go in (("up", z < 3), ("down", z > 0)):
            row, here = origin(hop, way)
            block = rows(row * 2 + x)
            wait((name, way, hop - 1), block, way, here)
            if hop < 3:
                send((name, way, hop), block, block, way, jnp.logical_and(here, go))
            send((name, "x", way, hop), block, block, "x", here)

    def wide_rest(name):
        _, rows = wide[name]
        placed[name].wait()
        for hop, way in spots:
            row, here = origin(hop, way)
            tag = (name, "x", 0) if hop == 0 else (name, "x", way, hop)
            wait(tag, rows(row * 2 + 1 - x), "x", here)

    wide_own("w01")
    for hop, way in spots:
        row, here = origin(hop, way)
        for name, _, out in small:
            tag = (name, "x", 0) if hop == 0 else (name, "x", way, hop)
            block = out.at[row * 2 + 1 - x, seq]
            wait(tag, block, "x", here)
            for kind in ("y", "core"):
                send((name, kind, "x", way, hop), block, block, kind, here)
    bias(2)
    bias(3)
    for hop, way in spots:
        row, here = origin(hop, way)
        for name, _, out in small:
            tag = (name, "y", 0) if hop == 0 else (name, "y", way, hop)
            block = out.at[row * 2 + x, s_y]
            wait(tag, block, "y", here)
            send((name, "relay", "own", way, hop), block, block, "core", here)
    bias(4)
    bias(5)
    wide_hop("w01", 1)
    for hop, way in spots:
        row, here = origin(hop, way)
        for name, _, out in small:
            block = out.at[row * 2 + 1 - x, s_y]
            wait((name, "y", "x", way, hop), block, "y", here)
            send((name, "relay", "x", way, hop), block, block, "core", here)

    def core_rest(which):
        for hop, way in spots:
            row, here = origin(hop, way)
            for name, _, out in small:
                if name == which:
                    tag = (name, "core", 0) if hop == 0 else (name, "core", way, hop)
                    wait(tag, out.at[row * 2 + x, s_core], "core", here)
                    wait((name, "core", "x", way, hop), out.at[row * 2 + 1 - x, s_core], "core", here)
                    wait((name, "relay", "own", way, hop), out.at[row * 2 + x, s_diag], "core", here)
                    wait((name, "relay", "x", way, hop), out.at[row * 2 + 1 - x, s_diag], "core", here)

    core_rest("qkv")
    for i in range(32):
        wqkv[46 * i : 46 * i + 46, :] = oqkv[i // 4, i % 4]
    mail.keep(wqkv, wqkv_out, keep_sems.at[2])
    kv_own[...] = dot_nn(normed_one, wqkv[:, INNER:]).astype(low)
    kv_all[seq] = kv_own[...]
    send("kvc", kv_own, kv_all.at[seq], "core")
    send("kvy", kv_own, kv_all.at[seq], "y")
    query[...] = dot_nn(normed_one, wqkv[:, :INNER]).astype(low)
    mail.keep(query, q_out, keep_sems.at[3])
    core_rest("wo")
    for i in range(32):
        wo[12 * i : 12 * i + 12, :] = owo[i // 4, i % 4]
    mail.keep(wo, wo_out, keep_sems.at[4])
    wide_hop("w01", 2)
    wait("kvy", kv_all.at[s_y], "y")
    send("kvr", kv_all.at[s_y], kv_all.at[s_y], "core")
    wait("kvc", kv_all.at[s_core], "core")
    wait("kvr", kv_all.at[s_diag], "core")
    mail.keep(kv_all, kv_out, keep_sems.at[5])

    lane = lax.broadcasted_iota(jnp.int32, (256, 128), 1)
    for pair in range(3):
        left = 128 * pair
        keys = kv_all[:, :, left : left + 128].reshape(1024, 128)
        values = kv_all[:, :, INNER + left : INNER + left + 128].reshape(1024, 128)
        both = query[:, left : left + 128]
        parts = []
        for side in range(2):
            head = 2 * pair + side
            mine = (lane < 64) if side == 0 else (lane >= 64)
            part = jnp.where(mine, both, jnp.zeros_like(both))
            scores = dot_nt(part, keys) + probs[head]
            expo = jnp.exp(scores - jnp.max(scores, axis=-1, keepdims=True))
            share = expo * (1.0 / jnp.sum(expo, axis=-1, keepdims=True))
            probs[head] = share
            parts.append(dot_nn(share.astype(low), values))
        mixed[:, left : left + 128] = jnp.where(lane < 64, parts[0], parts[1]).astype(low)
        if pair == 0:
            wide_hop("w01", 3)
            wide_own("w2")
    mail.keep(probs, p_out, keep_sems.at[6])
    mail.keep(mixed, mixed_out, keep_sems.at[7])
    wide_hop("w2", 1)
    h1[...] = x_in[...].astype(full) + dot_nn(mixed[...], wo[...])
    mail.keep(h1, h1_out, keep_sems.at[8])
    after_attn = h1[...]
    scale_two = norm_scale(after_attn)
    n2_own[...] = (after_attn * scale_two * gain_two[...]).astype(low)
    send("n2y", n2_own, n2_all.at[seq], "y")
    send("n2c", n2_own, n2_all.at[seq], "core")
    n2_all[seq] = n2_own[...]
    wide_hop("w2", 2)
    wide_rest("w01")
    mail.keep(w01, w01_out, keep_sems.at[9])

    def up_block(i):
        at = ((y + i // 2) % 2) * 2 + (core + i % 2) % 2
        tokens = n2_all[at]
        gate_pre = dot_nn(tokens, w01[:, : FF // 4])
        up_pre = dot_nn(tokens, w01[:, FF // 4 :])
        pre[at, 0] = gate_pre
        pre[at, 1] = up_pre
        hidden[at] = (gelu_tanh(gate_pre) * up_pre).astype(low)

    up_block(0)
    wait("n2c", n2_all.at[s_core], "core")
    wait("n2y", n2_all.at[s_y], "y")
    send("n2r", n2_all.at[s_y], n2_all.at[s_y], "core")
    wide_hop("w2", 3)
    wait("n2r", n2_all.at[s_diag], "core")

    def rest(i, carry):
        up_block(i)
        return carry

    lax.fori_loop(1, 4, rest, 0)
    mail.keep(pre, pre_out, keep_sems.at[11])
    for at in range(4):
        n2_t[:, 256 * at : 256 * at + 256] = n2_all[at].T
        hid_t[:, 256 * at : 256 * at + 256] = hidden[at].T
    mail.keep(n2_t, n2t_out, keep_sems.at[10])
    mail.keep(hid_t, hidt_out, keep_sems.at[12])
    wide_rest("w2")
    mail.keep(w2, w2_out, keep_sems.at[13])
    fsend[0] = dot_nn(hidden[s_diag], w2[...]).astype(low)
    send(("f", 0), fsend.at[0], frecv.at[0], "core")
    far = dot_nn(hidden[s_y], w2[...])
    wait(("f", 0), frecv.at[0], "core")
    fysend[...] = (far + frecv[0].astype(full)).astype(low)
    send("fy", fysend, fyrecv, "y")
    fsend[1] = dot_nn(hidden[s_core], w2[...]).astype(low)
    send(("f", 1), fsend.at[1], frecv.at[1], "core")
    h2[...] = h1[...] + dot_nn(hidden[seq], w2[...])
    wait(("f", 1), frecv.at[1], "core")
    wait("fy", fyrecv, "y")
    h2[...] = h2[...] + (frecv[1].astype(full) + fyrecv[...].astype(full))
    mail.keep(h2, h2_out, keep_sems.at[14])
    mail.finish()


def forward_all(x_in, qdoc, kdoc, window, gain_one, gain_two, a01, a2, aqkv, awo):
    low, full = jnp.bfloat16, jnp.float32
    here = pl.BlockSpec(memory_space=pltpu.VMEM)
    away = pl.BlockSpec(memory_space=pl.ANY)
    half = FF // 4
    outs = (
        ((D, 2 * half), low), ((half, D), low), ((D, 3 * INNER), low), ((INNER, D), low),
        ((256, INNER), low), ((4, 256, 2 * INNER), low), ((HEADS, 256, 1024), full),
        ((256, INNER), low), ((256, D), full), ((D, 1024), low),
        ((4, 2, 256, half), full), ((half, 1024), low), ((256, D), full),
    )
    scratch = (
        ((4, 46, 2 * half), low), ((184, 2 * half), low), ((D, 2 * half), low), ((half, D), low),
        ((8, 4, 46, 3 * INNER), low), ((D, 3 * INNER), low), ((8, 4, 12, D), low), ((INNER, D), low),
        ((HEADS, 256, 1024), full), ((256, INNER), low), ((256, 2 * INNER), low),
        ((4, 256, 2 * INNER), low), ((256, INNER), low), ((256, D), full), ((256, D), low),
        ((4, 256, D), low), ((D, 1024), low), ((4, 2, 256, half), full), ((4, 256, half), low),
        ((half, 1024), low), ((2, 256, D), low), ((2, 256, D), low), ((256, D), low), ((256, D), low), ((256, D), full),
    )
    return pl.pallas_call(
        forward_kernel,
        out_shape=tuple(jax.ShapeDtypeStruct(s, t) for s, t in outs),
        in_specs=[here] * 10,
        out_specs=(away,) * len(outs),
        scratch_shapes=[pltpu.VMEM(s, t) for s, t in scratch]
        + [
            pltpu.SemaphoreType.DMA((160,)),
            pltpu.SemaphoreType.DMA((160,)),
            pltpu.SemaphoreType.DMA((16,)),
        ],
        compiler_params=pltpu.CompilerParams(
            collective_id=0, has_side_effects=True, vmem_limit_bytes=67043328
        ),
        name="forward_all",
    )(x_in, qdoc, kdoc, window, gain_one, gain_two, a01, a2, aqkv, awo)


def middle_kernel(
    outcot, h2_in, h1_in, gatecot, gain_two, gain_three, d_weight, d_bias,
    w2_hbm, w01_hbm, pre_hbm, hid_hbm, n2t_hbm,
    block_out, gate_out, dh1_out, sums_out, g01_out, g2_out,
    w2, w01, pre, hid_t, n2_t, branch, branch_all, du, own_part, resid,
    fsend, frecv, fysend, fyrecv, g01, g2, send_sems, recv_sems, keep_sems,
):
    low, full = jnp.bfloat16, jnp.float32
    half = FF // 4
    net = Links(send_sems, recv_sems)
    mail = Mail(net)
    send, wait = mail.send, mail.wait
    seq, y, core = net.seq, net.y, net.core
    s_core, s_y, s_diag = y * 2 + 1 - core, (1 - y) * 2 + core, (1 - y) * 2 + 1 - core
    loads = [
        pltpu.make_async_copy(src, dst, keep_sems.at[i])
        for i, (src, dst) in enumerate(
            ((w2_hbm, w2), (pre_hbm, pre), (w01_hbm, w01), (hid_hbm, hid_t), (n2t_hbm, n2_t))
        )
    ]
    for made in loads:
        made.start()
    net.greet(("y", "core"))

    after = h2_in[...]
    block_out[...] = after.astype(low)
    scale = norm_scale(after)
    normed = after * scale * gain_three[...]
    logits = jnp.sum(normed * d_weight[...], axis=-1, keepdims=True) + d_bias[...]
    sigmoid = jax.nn.sigmoid(logits)
    gate_out[...] = DEPTH * sigmoid
    logit_grad = gatecot[...] * DEPTH * sigmoid * (1.0 - sigmoid)
    normed_grad = logit_grad * d_weight[...]
    sums_out[0:1, :] = jnp.sum(normed_grad * after * scale, axis=0, keepdims=True)
    sums_out[1:2, :] = jnp.sum(logit_grad * normed, axis=0, keepdims=True)
    sums_out[3:4, :] = jnp.broadcast_to(jnp.sum(logit_grad, axis=0, keepdims=True), (1, D))
    resid[...] = outcot[...].astype(full) + norm_back(after, scale, gain_three[...], normed_grad)
    branch[...] = resid[...].astype(low)
    send("by", branch, branch_all.at[seq], "y")
    send("bc", branch, branch_all.at[seq], "core")
    branch_all[seq] = branch[...]
    for made in loads[:3]:
        made.wait()

    def back_block(at):
        hidden_grad = dot_nt(branch_all[at], w2[...])
        gate_pre = pre[at, 0]
        up_pre = pre[at, 1]
        tangent = jnp.tanh(SLOPE * (gate_pre + CUBIC * gate_pre * gate_pre * gate_pre))
        gelu = 0.5 * gate_pre * (1.0 + tangent)
        slope = 0.5 * (1.0 + tangent) + 0.5 * gate_pre * (1.0 - tangent * tangent) * SLOPE * (
            1.0 + 3.0 * CUBIC * gate_pre * gate_pre
        )
        du[at, :, :half] = (hidden_grad * up_pre * slope).astype(low)
        du[at, :, half:] = (hidden_grad * gelu).astype(low)
        return dot_nt(du[at], w01[...])

    own_part[...] = back_block(seq)
    wait("bc", branch_all.at[s_core], "core")
    fsend[1] = back_block(s_core).astype(low)
    send(("f", 1), fsend.at[1], frecv.at[1], "core")
    wait("by", branch_all.at[s_y], "y")
    send("br", branch_all.at[s_y], branch_all.at[s_y], "core")
    wait("br", branch_all.at[s_diag], "core")
    fsend[0] = back_block(s_diag).astype(low)
    send(("f", 0), fsend.at[0], frecv.at[0], "core")
    far = back_block(s_y)
    wait(("f", 0), frecv.at[0], "core")
    fysend[...] = (far + frecv[0].astype(full)).astype(low)
    send("fy", fysend, fyrecv, "y")

    for made in loads[3:]:
        made.wait()

    def down_columns(cols, width):
        part = dot_nn(hid_t[...], branch_all[:, :, cols].reshape(1024, width))
        for b in range(8):
            g2[b, :, cols] = part[112 * b : 112 * b + 112].astype(low)

    def down_step(i, carry):
        down_columns(pl.ds(pl.multiple_of(i * 256, 256), 256), 256)
        return carry

    lax.fori_loop(0, 5, down_step, 0)
    down_columns(slice(1280, D), D - 1280)
    mail.keep(g2, g2_out, keep_sems.at[5])

    def wide_step(i, carry):
        cols = pl.ds(pl.multiple_of(i * 256, 256), 256)
        part = dot_nn(n2_t[...], du[:, :, cols].reshape(1024, 256))
        for b in range(8):
            g01[b, :, cols] = part[184 * b : 184 * b + 184].astype(low)
        return carry

    lax.fori_loop(0, 7, wide_step, 0)
    mail.keep(g01, g01_out, keep_sems.at[6])

    wait(("f", 1), frecv.at[1], "core")
    wait("fy", fyrecv, "y")
    normed_two_grad = own_part[...] + (frecv[1].astype(full) + fyrecv[...].astype(full))
    before = h1_in[...]
    scale_two = norm_scale(before)
    sums_out[2:3, :] = jnp.sum(normed_two_grad * before * scale_two, axis=0, keepdims=True)
    dh1_out[...] = resid[...] + norm_back(before, scale_two, gain_two[...], normed_two_grad)
    mail.finish()


def middle_all(outcot, h2, h1, gatecot, gain_two, gain_three, d_weight, d_bias, w2, w01, pre, hid_t, n2_t):
    low, full = jnp.bfloat16, jnp.float32
    here = pl.BlockSpec(memory_space=pltpu.VMEM)
    away = pl.BlockSpec(memory_space=pl.ANY)
    half = FF // 4
    grads = (((8, 184, 2 * half), low), ((8, 112, D), low))
    outs = (((256, D), low), ((256, 1), full), ((256, D), full), ((4, D), full)) + grads
    scratch = (
        ((half, D), low), ((D, 2 * half), low), ((4, 2, 256, half), full), ((half, 1024), low),
        ((D, 1024), low), ((256, D), low), ((4, 256, D), low), ((4, 256, 2 * half), low),
        ((256, D), full), ((256, D), full), ((2, 256, D), low), ((2, 256, D), low),
        ((256, D), low), ((256, D), low),
    ) + grads
    return pl.pallas_call(
        middle_kernel,
        out_shape=tuple(jax.ShapeDtypeStruct(s, t) for s, t in outs),
        in_specs=[here] * 8 + [away] * 5,
        out_specs=(here,) * 4 + (away,) * 2,
        scratch_shapes=[pltpu.VMEM(s, t) for s, t in scratch]
        + [
            pltpu.SemaphoreType.DMA((16,)),
            pltpu.SemaphoreType.DMA((16,)),
            pltpu.SemaphoreType.DMA((8,)),
        ],
        compiler_params=pltpu.CompilerParams(
            collective_id=1, has_side_effects=True, vmem_limit_bytes=67043328
        ),
        name="middle_all",
    )(outcot, h2, h1, gatecot, gain_two, gain_three, d_weight, d_bias, w2, w01, pre, hid_t, n2_t)


def backward_kernel(
    x_in, dh1_in, mixed, query, gain_one, hot, sums_in, g01, g2, kv_hbm, p_hbm, wqkv_hbm, wo_hbm,
    grad_out, r01, r2, rqkv, rwo, small_out,
    own01, own2, x01, x2, z01, z2, stage, kv_all, probs, wqkv, wo, n1_t, do_all, diag,
    dkv, ksend, krecv, kysend, kyrecv, dqkv, gqkv, gwo,
    cqkv, cwo, yqkv, ywo, xqkv, xwo, zqkv, zwo, acc, met,
    send_sems, recv_sems, keep_sems,
):
    low, full = jnp.bfloat16, jnp.float32
    net = Links(send_sems, recv_sems)
    mail = Mail(net)
    send, wait = mail.send, mail.wait
    dp, seq, z, x, y, core = net.dp, net.seq, net.z, net.x, net.y, net.core
    s_core, s_y, s_diag = y * 2 + 1 - core, (1 - y) * 2 + core, (1 - y) * 2 + 1 - core
    seats = (("core", s_core), ("y", s_y), ("diag", s_diag))
    spots = [(h, w) for h in (3, 2, 1) for w in ("up", "down")] + [(0, "up")]
    loads = {}

    def load(name, src, dst):
        loads[name] = pltpu.make_async_copy(src, dst, keep_sems.at[len(loads)])
        loads[name].start()

    load("wo", wo_hbm, wo)
    load("kv", kv_hbm, kv_all)
    load("p", p_hbm, probs)
    load("wqkv", wqkv_hbm, wqkv)
    for row in range(4):
        load(("g2", row), g2.at[row * 2 + x], own2.at[row])
        load(("g01", row), g01.at[row * 2 + x], own01.at[row])
    net.greet(("y", "core", "diag"), far=True)

    def target(hop, way):
        here = None if hop == 0 else (z + hop <= 3 if way == "up" else z >= hop)
        return jnp.clip(z + (hop if way == "up" else -hop), 0, 3), here

    wide = (("w2", g2, own2, x2, z2), ("w01", g01, own01, x01, z01))
    for hop, way in spots:
        row, here = target(hop, way)
        for name, grads, _, xin, _ in wide:
            send((name, "x", way, hop), grads.at[row * 2 + 1 - x], xin.at[row], "x", here)

    def add(to, plus):
        if len(to.shape) == 3:
            for i in range(to.shape[0]):
                to[i] = (to[i].astype(full) + plus[i].astype(full)).astype(low)
        else:
            to[...] = (to[...].astype(full) + plus[...].astype(full)).astype(low)

    def along_z(name, own, xin, zin, hop, way):
        row, here = target(hop, way)
        block = xin.at[row]

        def step():
            wait((name, "x", way, hop), block, "x")
            add(block, own(row))
            if hop == 0:
                for other, came, slot in (("up", z > 0, z), ("down", z < 3, 4)):

                    @pl.when(came)
                    def _(other=other, slot=slot):
                        wait((name, other, 1), zin.at[slot], other)
                        add(block, zin.at[slot])

            elif hop < 3:

                @pl.when(z > 0 if way == "up" else z < 3)
                def _():
                    wait((name, way, hop + 1), zin.at[row], way)
                    add(block, zin.at[row])

        if here is None:
            step()
        else:
            pl.when(here)(step)
        if hop:
            slot = row if way == "up" or hop > 1 else 4
            send((name, way, hop), block, zin.at[slot], way, here)

    def wide_rows(hop):
        for name, _, own, xin, zin in wide:
            for way in ("up", "down") if hop else ("up",):
                along_z(name, lambda row: own.at[row], xin, zin, hop, way)

    loads["wo"].wait()
    branch = dh1_in[...].astype(low)
    do_all[...] = dot_nt(branch, wo[...]).astype(low)
    out_grad = dot_tn(mixed[...], branch)
    for i in range(32):
        gwo[i // 4, i % 4] = out_grad[12 * i : 12 * i + 12].astype(low)
    narrow = (
        ("wo", gwo, cwo, ywo, xwo, zwo),
        ("qkv", gqkv, cqkv, yqkv, xqkv, zqkv),
    )

    def narrow_core(which):
        name, own, cin = narrow[which][:3]
        for d in range(8):
            for yy in range(2):
                send((name, "core", d, yy), own.at[d, yy * 2 + 1 - core], cin.at[d, yy], "core")

    def narrow_y(which):
        name, own, cin, yin = narrow[which][:4]
        for first in (True, False):
            for d in range(8):
                yy = 1 - y if first else y
                if first:
                    wait((name, "core", d, 0), cin.at[d, 0], "core")
                    wait((name, "core", d, 1), cin.at[d, 1], "core")
                add(cin.at[d, yy], own.at[d, yy * 2 + core])
                if first:
                    send((name, "y", d), cin.at[d, yy], yin.at[d], "y")

    def narrow_x(which):
        name, own, cin, yin, xin, zin = narrow[which]
        for d in range(8):
            wait((name, "y", d), yin.at[d], "y")
            add(cin.at[d, y], yin.at[d])
        for hop, way in spots:
            row, here = target(hop, way)
            send((name, "x", way, hop), cin.at[row * 2 + 1 - x, y], xin.at[row], "x", here)

    narrow_core(0)
    inputs = x_in[...].astype(full)
    scale_one = norm_scale(inputs)
    n1_t[...] = (inputs * scale_one * gain_one[...]).astype(low).T
    narrow_y(0)
    loads["kv"].wait()
    loads["p"].wait()
    loads["wqkv"].wait()

    lane = lax.broadcasted_iota(jnp.int32, (256, 128), 1)
    blank = jnp.zeros((8, 256), full)
    for pair in range(3):
        left = 128 * pair
        keys = kv_all[:, :, left : left + 128].reshape(1024, 128)
        values = kv_all[:, :, INNER + left : INNER + left + 128].reshape(1024, 128)
        asks = query[:, left : left + 128]
        outs = do_all[:, left : left + 128]
        key_terms = value_terms = None
        parts = []
        for side in range(2):
            head = 2 * pair + side
            mine = (lane < 64) if side == 0 else (lane >= 64)
            out_part = jnp.where(mine, outs, jnp.zeros_like(outs))
            ask_part = jnp.where(mine, asks, jnp.zeros_like(asks))
            share_grad = dot_nt(out_part, values)
            share = probs[head]
            value_part = dot_tn(share.astype(low), out_part)
            score_grad = share * (
                share_grad - jnp.sum(share * share_grad, axis=-1, keepdims=True)
            )
            probs[head] = score_grad
            score_low = score_grad.astype(low)
            parts.append(dot_nn(score_low, keys))
            key_part = dot_tn(score_low, ask_part)
            key_terms = key_part if side == 0 else key_terms + key_part
            value_terms = value_part if side == 0 else value_terms + value_part
        dqkv[:, left : left + 128] = jnp.where(lane < 64, parts[0], parts[1]).astype(low)
        dkv[:, :, left : left + 128] = key_terms.astype(low).reshape(4, 256, 128)
        dkv[:, :, INNER + left : INNER + left + 128] = value_terms.astype(low).reshape(4, 256, 128)
        if pair == 0:
            narrow_x(0)
        if pair == 1:
            for row in range(4):
                loads[("g2", row)].wait()
                loads[("g01", row)].wait()
            wide_rows(3)

    ksend[0] = dkv[s_diag]
    ksend[1] = dkv[s_core]
    send(("k", 0), ksend.at[0], krecv.at[0], "core")
    send(("k", 1), ksend.at[1], krecv.at[1], "core")
    wait(("k", 0), krecv.at[0], "core")
    kysend[...] = (dkv[s_y].astype(full) + krecv[0].astype(full)).astype(low)
    send("ky", kysend, kyrecv, "y")

    diag[:, HEADS:, :] = jnp.zeros((8, 8 - HEADS, 1280), full)
    for head in range(HEADS):
        total = jnp.zeros((8, 1280), full)
        for g in range(32):
            piece = jnp.concatenate([blank, probs[head, 8 * g : 8 * g + 8, :]], axis=1)
            total = total + (pltpu.roll(piece, 1280 - 8 * g, 1) if g else piece)
        diag[:, head, :] = total
    line = diag[0]
    for i in range(1, 8):
        line = line + pltpu.roll(diag[i], 1280 - i, 1)
    table = jnp.dot(line, hot[...], precision=HIGH, preferred_element_type=full)

    query_part = dot_nn(n1_t[...], dqkv[:, :INNER])

    def place(part, which):
        for i in range(32):
            gqkv[i // 4, i % 4, :, which * INNER : which * INNER + INNER] = part[
                46 * i : 46 * i + 46
            ].astype(low)

    place(query_part, 0)
    wait(("k", 1), krecv.at[1], "core")
    wait("ky", kyrecv, "y")
    dqkv[:, INNER:] = (
        dkv[seq].astype(full) + (krecv[1].astype(full) + kyrecv[...].astype(full))
    ).astype(low)
    for which in (1, 2):
        place(dot_nn(n1_t[...], dqkv[:, which * INNER : which * INNER + INNER]), which)
    narrow_core(1)
    normed_grad = dot_nt(dqkv[...], wqkv[...])
    grad_out[...] = dh1_in[...] + norm_back(inputs, scale_one, gain_one[...], normed_grad)
    acc[0, 0:1, :] = jnp.sum(normed_grad * inputs * scale_one, axis=0, keepdims=True)
    acc[0, 1:5, :] = sums_in[...]
    acc[0, 5:8, :] = jnp.zeros((3, D), full)
    acc[0, 8:16, 0:128] = table
    acc[0, 8:16, 128:] = jnp.zeros((8, D - 128), full)
    narrow_y(1)
    steps = (("core", None), ("y", None), ("x", None), ("z1", None), ("z2", None))

    def small_step(i):
        kind = steps[i][0]
        if i:
            before = steps[i - 1][0]
            wait(("sum", i - 1), met.at[i - 1], before)
            acc[i] = acc[i - 1] + met[i - 1]
        send(("sum", i), acc.at[i], met.at[i], kind)

    small_step(0)
    wide_rows(2)
    small_step(1)
    narrow_x(1)
    small_step(2)
    wide_rows(1)
    small_step(3)
    wide_rows(0)
    small_step(4)
    for s in range(4):
        stage[s] = x01[z, 46 * s : 46 * s + 46, :]
    for kind, slot in seats:
        send(("a2a", kind), stage.at[slot], r01.at[seq], kind)
    r01[seq] = stage[seq]
    r2[...] = x2[z]
    for hop in (3, 2, 1, 0):
        for name, own, cin, yin, xin, zin in narrow:
            for way in ("up", "down") if hop else ("up",):
                along_z(name, lambda row: cin.at[row * 2 + x, y], xin, zin, hop, way)
    rqkv[...] = xqkv[z]
    rwo[...] = xwo[z]
    wait(("sum", 4), met.at[4], "z2")
    small_out[...] = acc[4] + met[4]
    for kind, slot in seats:
        wait(("a2a", kind), r01.at[slot], kind)
    mail.finish()


def backward_all(x_in, dh1, mixed, query, gain_one, hot, sums, g01, g2, kv_all, probs, wqkv, wo):
    low, full = jnp.bfloat16, jnp.float32
    here = pl.BlockSpec(memory_space=pltpu.VMEM)
    away = pl.BlockSpec(memory_space=pl.ANY)
    wide = 2 * (FF // 4)
    outs = (
        ((256, D), full), ((4, 46, wide), low), ((112, D), low),
        ((46, 3 * INNER), low), ((12, D), low), ((16, D), full),
    )
    qkv, out = (46, 3 * INNER), (12, D)
    scratch = (
        ((4, 184, wide), low), ((4, 112, D), low), ((4, 184, wide), low), ((4, 112, D), low),
        ((5, 184, wide), low), ((5, 112, D), low), ((4, 46, wide), low),
        ((4, 256, 2 * INNER), low), ((HEADS, 256, 1024), full), ((D, 3 * INNER), low),
        ((INNER, D), low), ((D, 256), low), ((256, INNER), low), ((8, 8, 1280), full),
        ((4, 256, 2 * INNER), low), ((2, 256, 2 * INNER), low), ((2, 256, 2 * INNER), low),
        ((256, 2 * INNER), low), ((256, 2 * INNER), low), ((256, 3 * INNER), low),
        ((8, 4) + qkv, low), ((8, 4) + out, low), ((8, 2) + qkv, low), ((8, 2) + out, low),
        ((8,) + qkv, low), ((8,) + out, low), ((4,) + qkv, low), ((4,) + out, low),
        ((5,) + qkv, low), ((5,) + out, low), ((5, 16, D), full), ((5, 16, D), full),
    )
    return pl.pallas_call(
        backward_kernel,
        out_shape=tuple(jax.ShapeDtypeStruct(s, t) for s, t in outs),
        in_specs=[here] * 7 + [away] * 6,
        out_specs=(here,) * 6,
        scratch_shapes=[pltpu.VMEM(s, t) for s, t in scratch]
        + [
            pltpu.SemaphoreType.DMA((160,)),
            pltpu.SemaphoreType.DMA((160,)),
            pltpu.SemaphoreType.DMA((12,)),
        ],
        compiler_params=pltpu.CompilerParams(
            collective_id=2, has_side_effects=True, vmem_limit_bytes=67043328
        ),
        name="backward_all",
    )(x_in, dh1, mixed, query, gain_one, hot, sums, g01, g2, kv_all, probs, wqkv, wo)


def local_rows(
    block_input, segment_ids, attention_gain, query_weight, key_weight, value_weight,
    output_weight, bias_table, feedforward_gain, gelu_weight, up_weight, down_weight,
    delete_gain, delete_weight, delete_bias, output_cotangent, gate_cotangent,
):
    low, full = jnp.bfloat16, jnp.float32
    seq_length = segment_ids.shape[1]
    tokens = block_input.shape[1]
    offset = lax.axis_index("seq") * tokens
    half = FF // 4

    def by_column(flat):
        return flat.reshape(46, 8, 4, 112).transpose(2, 0, 1, 3).reshape(4, 46, half)

    a01 = jnp.concatenate([by_column(gelu_weight), by_column(up_weight)], axis=2)
    aqkv = jnp.concatenate(
        [w.reshape(46, INNER) for w in (query_weight, key_weight, value_weight)], axis=1
    )
    spread = np.pad(relative_buckets(seq_length, BUCKETS, MAX_DIST), (1, 0))
    near = lax.dynamic_slice_in_dim(jnp.asarray(spread), seq_length - 256 - offset, 1280)
    one_hot = (near[:, None] == lax.iota(jnp.int32, 128)[None, :]).astype(full)
    table = jnp.pad(bias_table, ((0, 128 - BUCKETS), (0, 8 - HEADS)))
    window = jnp.einsum("jb,bh->hj", one_hot, table, precision=HIGH)
    query_docs = lax.dynamic_slice_in_dim(segment_ids, offset, tokens, 1)
    block_input = block_input.reshape(tokens, D)
    gain_one = attention_gain.reshape(1, D)
    gain_two = feedforward_gain.reshape(1, D)
    (
        w01, w2, wqkv, wo, query, kv_all, probs, mixed, h1, n2_t, pre, hid_t, h2,
    ) = forward_all(
        block_input, query_docs.reshape(tokens, 1), segment_ids, window, gain_one, gain_two,
        a01, down_weight.reshape(112, D), aqkv, output_weight.reshape(12, D),
    )
    block_output, delete_gate, dh1, sums, g01, g2 = middle_all(
        output_cotangent.reshape(tokens, D), h2, h1, gate_cotangent.reshape(tokens, 1),
        gain_two, delete_gain.reshape(1, D), delete_weight.reshape(1, D),
        delete_bias.reshape(1, 1), w2, w01, pre, hid_t, n2_t,
    )
    input_gradient, r01, r2, rqkv, rwo, small = backward_all(
        block_input, dh1, mixed, query, gain_one, one_hot, sums, g01, g2, kv_all, probs, wqkv, wo
    )

    def by_row(cols):
        return (
            cols.astype(full).reshape(4, 46, 8, 112).transpose(1, 2, 0, 3).reshape(46 * FF)
        )

    narrow = rqkv.astype(full)
    return (
        block_output.reshape(1, tokens, D),
        delete_gate.reshape(1, tokens),
        input_gradient.reshape(1, tokens, D),
        small[0],
        narrow[:, :INNER].reshape(-1),
        narrow[:, INNER : 2 * INNER].reshape(-1),
        narrow[:, 2 * INNER :].reshape(-1),
        rwo.astype(full).reshape(-1),
        small[8 : 8 + HEADS, :BUCKETS].T,
        small[3],
        by_row(r01[:, :, :half]),
        by_row(r01[:, :, half:]),
        r2.astype(full).reshape(-1),
        small[1],
        small[2],
        small[4, :1],
    )


def solution(mesh):
    placed = (
        P("dp", "seq", None),
        P("dp", None),
        P(),
        P(("dp", "seq")),
        P(("dp", "seq")),
        P(("dp", "seq")),
        P(("dp", "seq")),
        P(),
        P(),
        P(("dp", "seq")),
        P(("dp", "seq")),
        P(("dp", "seq")),
        P(),
        P(),
        P(),
        P("dp", "seq", None),
        P("dp", "seq"),
    )
    fast = mesh.shape["dp"] == 8 and mesh.shape["seq"] == 4
    return jax.shard_map(
        local_rows if fast else local,
        mesh=mesh,
        in_specs=placed,
        out_specs=(
            P("dp", "seq", None),
            P("dp", "seq"),
            P("dp", "seq", None),
            P(),
            P(("dp", "seq")),
            P(("dp", "seq")),
            P(("dp", "seq")),
            P(("dp", "seq")),
            P(),
            P(),
            P(("dp", "seq")),
            P(("dp", "seq")),
            P(("dp", "seq")),
            P(),
            P(),
            P(),
        ),
        check_vma=False,
    )
```
